32 devices in a mesh: dp: 8 (over z, x), tensor: 4 (over y, core).
Axes of the slice: x: 2, y: 2, z: 4, core: 2. Of those that a mesh axis runs over, the one named last changes fastest.
Arguments:
- layer_input: bfloat16 [12288, 768], P('dp'), may hold values from -6 to 6
- patch_coords: int32 [3, 12288], P(None, 'dp'), may hold values from 0 to 55, as said below
- item_lengths: int32 [32], P('dp'), may hold values from 0 to 1536, as said below
- out_grad: bfloat16 [12288, 768], P('dp'), may hold values from -6 to 6
- ln1_gain: bfloat16 [768], replicated, may hold values from 0.25 to 1.75
- ln1_shift: bfloat16 [768], replicated, may hold values from -1.75 to 1.75
- w_qkv: bfloat16 [768, 3, 768], P(None, None, 'tensor'), may hold values from -0.21875 to 0.21875
- b_qv: bfloat16 [2, 768], P(None, 'tensor'), may hold values from -3 to 3
- w_out: bfloat16 [768, 768], P('tensor'), may hold values from -0.875 to 0.875
- b_out: bfloat16 [768], replicated, may hold values from -1.75 to 1.75
- ln2_gain: bfloat16 [768], replicated, may hold values from 0.25 to 1.75
- ln2_shift: bfloat16 [768], replicated, may hold values from -1.75 to 1.75
- w_fc1: bfloat16 [768, 3072], P(None, 'tensor'), may hold values from -0.21875 to 0.21875
- b_fc1: bfloat16 [3072], P('tensor'), may hold values from -3 to 3
- w_fc2: bfloat16 [3072, 768], P('tensor'), may hold values from -0.109375 to 0.109375
- b_fc2: bfloat16 [768], replicated, may hold values from -1.75 to 1.75
Outputs:
- layer_output: bfloat16 [12288, 768], P('dp')
- input_grad: float32 [12288, 768], P('dp')
- grad_ln1_gain: float32 [768], replicated
- grad_ln1_shift: float32 [768], replicated
- grad_w_qkv: float32 [768, 3, 768], P(None, None, 'tensor')
- grad_b_qv: float32 [2, 768], P(None, 'tensor')
- grad_w_out: float32 [768, 768], P('tensor')
- grad_b_out: float32 [768], replicated
- grad_ln2_gain: float32 [768], replicated
- grad_ln2_shift: float32 [768], replicated
- grad_w_fc1: float32 [768, 3072], P(None, 'tensor')
- grad_b_fc1: float32 [3072], P('tensor')
- grad_w_fc2: float32 [3072, 768], P('tensor')
- grad_b_fc2: float32 [768], replicated
The draws below stay inside these ranges and needn't reach their ends.
Inputs may be any that keep to these rules, and one draw needn't show every extreme that they name: `item_lengths`: A row of 8 takes 4 consecutive entries: its items' visible lengths, laid out one after another from the row's first slot, summing to at most 1536; the remaining slots are padding. In every draw some row holds a single item of 1536 tokens. `patch_coords`: row 0 is the token's frame, 0 to 2; rows 1 and 2 are its patch row and column.
All inputs are finite; a program needn't handle non-finite values.
Results may differ from the reference program's by a relative error of at most 0.018.
Values may be sent and summed in bfloat16 or wider, within the bound.
A program may use at most 128 MiB of HBM per device.

```python
import math
import jax
import jax.numpy as jnp
from jax import lax

D = 768
HEADS = 12
HEAD_DIM = 64
FF = 3072
TOK_DEV = 1536
SLOTS = 4
TOKENS = 12288
ALL_SLOTS = 32
N_TENSOR = 4


def draw_item_lengths(key, part):
    device_count = ALL_SLOTS // SLOTS
    base_lengths = jax.random.randint(jax.random.fold_in(key, 1), (device_count, SLOTS), 0, TOK_DEV // SLOTS + 1)
    full_device = jax.random.randint(jax.random.fold_in(key, 2), (), 0, device_count)
    rows_at = jnp.arange(device_count)[:, None]
    slots_at = jnp.arange(SLOTS)[None, :]
    single = jnp.where(slots_at == 0, TOK_DEV, 0)
    return jnp.where(rows_at == full_device, single, base_lengths).reshape(-1).astype(jnp.int32)


def draw_patch_coords(key, part):
    frames = jax.random.randint(jax.random.fold_in(key, 3), (1, TOKENS), 0, 3)
    places = jax.random.randint(jax.random.fold_in(key, 4), (2, TOKENS), 0, 56)
    return jnp.concatenate([frames, places], axis=0).astype(jnp.int32)


def level_of(own_key, dims, cuts, smallest, high):
    loudness, own = 1.0, jax.random.fold_in(own_key, 6)
    for position, shards_of in cuts:
        steps = jnp.exp(jax.random.uniform(jax.random.fold_in(own, position), (shards_of,), jnp.float32, smallest / len(cuts), high / len(cuts)))
        loudness = loudness * jnp.repeat(steps, dims[position] // shards_of).reshape([-1 if axis == position else 1 for axis in range(len(dims))])
    return loudness


def normal_values(rng, extent, scale, reach, shards=(), kind=jnp.bfloat16):
    values = jax.random.normal(rng, extent, jnp.float32) * scale
    if len(shards) > 0:
        values = level_of(rng, extent, shards, -0.22, 0.18) * values
    return jnp.clip(values, min=-reach, max=reach).astype(kind)


def setup_inputs(seed: int = 0) -> dict:
    keys = jax.random.split(jax.random.key(seed), 17)
    layer_input = normal_values(keys[0], (TOKENS, D), 1.0, 6.0, ((0, 8),))
    patch_coords = draw_patch_coords(jax.random.fold_in(keys[16], 71), 0)
    item_lengths = draw_item_lengths(jax.random.fold_in(keys[16], 71), 0)
    out_grad = normal_values(keys[3], (TOKENS, D), 1.0, 6.0, ((0, 8),))
    ln1_gain = jnp.clip(1.0 + 0.15 * jax.random.normal(keys[4], (D,), jnp.float32), 0.25, 1.75).astype(jnp.bfloat16)
    ln1_shift = normal_values(keys[5], (D,), 0.3, 1.75)
    w_qkv = normal_values(keys[6], (D, 3, D), D ** -0.5, 0.21875, ((2, 4),))
    b_qv = normal_values(keys[7], (2, D), 0.5, 3.0, ((1, 4),))
    w_out = normal_values(keys[8], (D, D), (D // 16) ** -0.5, 0.875, ((0, 4),))
    b_out = normal_values(keys[9], (D,), 0.3, 1.75)
    ln2_gain = jnp.clip(1.0 + 0.15 * jax.random.normal(keys[10], (D,), jnp.float32), 0.25, 1.75).astype(jnp.bfloat16)
    ln2_shift = normal_values(keys[11], (D,), 0.3, 1.75)
    w_fc1 = normal_values(keys[12], (D, FF), D ** -0.5, 0.21875, ((1, 4),))
    b_fc1 = normal_values(keys[13], (FF,), 0.5, 3.0, ((0, 4),))
    w_fc2 = normal_values(keys[14], (FF, D), FF ** -0.5, 0.109375, ((0, 4),))
    b_fc2 = normal_values(keys[15], (D,), 0.3, 1.75)
    return {"layer_input": layer_input, "patch_coords": patch_coords, "item_lengths": item_lengths, "out_grad": out_grad, "ln1_gain": ln1_gain, "ln1_shift": ln1_shift, "w_qkv": w_qkv, "b_qv": b_qv, "w_out": w_out, "b_out": b_out, "ln2_gain": ln2_gain, "ln2_shift": ln2_shift, "w_fc1": w_fc1, "b_fc1": b_fc1, "w_fc2": w_fc2, "b_fc2": b_fc2}


NORM_EPS = 1e-06
MASK_FILL = -1e+30

@jax.custom_vjp
def low(v):
    return lax.optimization_barrier(v.astype(jnp.bfloat16)).astype(jnp.float32)

@jax.custom_vjp
def low_back(v):
    return v

def low_keep(v):
    return (low(v), None)

def low_pass(kept, grad):
    return (grad,)

def back_keep(v):
    return (v, None)

def back_low(kept, grad):
    return (low(grad),)
low.defvjp(low_keep, low_pass)
low_back.defvjp(back_keep, back_low)

def rounded(values_in):
    return low_back(low(values_in))

def dense(left_side, right_side):
    return jnp.dot(left_side, right_side, precision=lax.Precision.HIGHEST)

def layer_norm(values_in, norm_gain, norm_shift):
    mean_row = lax.optimization_barrier(jnp.mean(values_in, axis=-1, keepdims=True))
    centred = values_in - mean_row
    spread = lax.optimization_barrier(jnp.mean(centred * centred, axis=-1, keepdims=True))
    return centred * lax.rsqrt(spread + NORM_EPS) * norm_gain + norm_shift

def sincos_table(coords, feature_count):
    half_width = feature_count // 6
    ladder = jnp.arange(half_width, dtype=jnp.float32) / half_width
    frequency = jnp.power(10000.0, -ladder)
    angles = coords.astype(jnp.float32)[:, :, None] * frequency[None, None, :]
    wave_parts = jnp.concatenate([jnp.sin(angles), jnp.cos(angles)], axis=2)
    return jnp.concatenate([wave_parts[0], wave_parts[1], wave_parts[2]], axis=1)

def item_layout(length_rows, token_count, slot_count):
    item_ends = jnp.cumsum(length_rows, axis=1, dtype=jnp.int32)
    places = jnp.arange(token_count, dtype=jnp.int32)
    passed = (places[None, :, None] >= item_ends[:, None, :]).astype(jnp.int32)
    item_of = lax.optimization_barrier(jnp.sum(passed, axis=2, dtype=jnp.int32))
    visible = places[None, :] < item_ends[:, -1:]
    return (jnp.where(visible, item_of, slot_count + places[None, :]), visible)

def attend(query_rows, key_rows, value_rows, segment):
    score_scale = 1.0 / math.sqrt(query_rows.shape[2])
    scores = jnp.einsum('qhd,khd->hqk', query_rows, key_rows, precision=lax.Precision.HIGHEST) * score_scale
    scores = low_back(scores)
    allowed = (segment[:, None] == segment[None, :])[None]
    weights = jax.nn.softmax(jnp.where(allowed, scores, MASK_FILL), axis=2)
    return jnp.einsum('hqk,khd->qhd', low(weights), value_rows, precision=lax.Precision.HIGHEST)

def attend_packed(packed):
    return attend(packed[0], packed[1], packed[2], packed[3])

def forward(layer_in, pos_table, segment, visible, ln1_gain, ln1_shift, w_qkv, b_qv, w_out, b_out, ln2_gain, ln2_shift, w_fc1, b_fc1, w_fc2, b_fc2):
    tokens_all = layer_in.shape[0]
    groups = N_TENSOR
    hidden_in = layer_in + pos_table
    normed_one = low(layer_norm(hidden_in, ln1_gain, ln1_shift))
    query_rows = rounded(dense(normed_one, w_qkv[:, 0, :]) + b_qv[0])
    key_rows = rounded(dense(normed_one, w_qkv[:, 1, :]))
    value_rows = rounded(dense(normed_one, w_qkv[:, 2, :]) + b_qv[1])
    buffer_shape = (tokens_all // TOK_DEV, TOK_DEV, HEADS, HEAD_DIM)
    mixed = lax.map(jax.checkpoint(attend_packed), (query_rows.reshape(buffer_shape), key_rows.reshape(buffer_shape), value_rows.reshape(buffer_shape), segment))
    mixed = rounded(mixed.reshape(tokens_all, D))
    attn_parts = rounded(jnp.einsum('tgk,gkd->tgd', mixed.reshape(tokens_all, groups, D // groups), w_out.reshape(groups, D // groups, D), precision=lax.Precision.HIGHEST))
    middle = hidden_in + lax.optimization_barrier(jnp.sum(attn_parts, axis=1)) + b_out
    normed_two = low(layer_norm(middle, ln2_gain, ln2_shift))
    hidden_pre = low_back(dense(normed_two, w_fc1) + b_fc1)
    activated = low(jax.nn.gelu(hidden_pre, approximate=False))
    mlp_parts = rounded(jnp.einsum('tgk,gkd->tgd', activated.reshape(tokens_all, groups, FF // groups), w_fc2.reshape(groups, FF // groups, D), precision=lax.Precision.HIGHEST))
    return jnp.where(visible.reshape(-1)[:, None], middle + lax.optimization_barrier(jnp.sum(mlp_parts, axis=1)) + b_fc2, 0.0)

def reference(layer_input, patch_coords, item_lengths, out_grad, ln1_gain, ln1_shift, w_qkv, b_qv, w_out, b_out, ln2_gain, ln2_shift, w_fc1, b_fc1, w_fc2, b_fc2):
    segment, visible = item_layout(item_lengths.reshape(-1, SLOTS), TOK_DEV, SLOTS)
    pos_table = sincos_table(patch_coords, D)
    floats = [layer_input, ln1_gain, ln1_shift, w_qkv, b_qv, w_out, b_out, ln2_gain, ln2_shift, w_fc1, b_fc1, w_fc2, b_fc2]
    floats = [entry.astype(jnp.float32) for entry in floats]

    def forward_tied(*pieces):
        return forward(pieces[0], pos_table, segment, visible, *pieces[1:])
    result, pullback = jax.vjp(forward_tied, *floats)
    gradients = pullback(out_grad.astype(jnp.float32))
    return (result.astype(jnp.bfloat16), gradients[0], gradients[1], gradients[2], gradients[3], gradients[4], gradients[5], gradients[6], gradients[7], gradients[8], gradients[9], gradients[10], gradients[11], gradients[12])
```

```python
from functools import partial
import math

import jax
import jax.numpy as jnp
from jax import lax
from jax.sharding import PartitionSpec as P

HEAD_DIM = 64


NORM_EPS = 1e-06
MASK_FILL = -1e30


def layer_norm(values_in, norm_gain, norm_shift):
    mean_row = jnp.mean(values_in, axis=-1, keepdims=True)
    centred = values_in - mean_row
    spread = jnp.mean(centred * centred, axis=-1, keepdims=True)
    return centred * lax.rsqrt(spread + NORM_EPS) * norm_gain + norm_shift


def sincos_table(coords, feature_count):
    half_width = feature_count // 6
    ladder = jnp.arange(half_width, dtype=jnp.float32) / half_width
    frequency = jnp.power(10000.0, -ladder)
    angles = coords.astype(jnp.float32)[:, :, None] * frequency[None, None, :]
    wave_parts = jnp.concatenate([jnp.sin(angles), jnp.cos(angles)], axis=2)
    return jnp.concatenate([wave_parts[0], wave_parts[1], wave_parts[2]], axis=1)


def item_layout(length_rows, token_count, slot_count):
    item_ends = jnp.cumsum(length_rows, axis=1, dtype=jnp.int32)
    places = jnp.arange(token_count, dtype=jnp.int32)
    passed = (places[None, :, None] >= item_ends[:, None, :]).astype(jnp.int32)
    item_of = jnp.sum(passed, axis=2, dtype=jnp.int32)
    visible = places[None, :] < item_ends[:, -1:]
    return (jnp.where(visible, item_of, slot_count + places[None, :]), visible)


def block_scores(query_block, key_rows, segment_block, segment):
    score_scale = 1.0 / math.sqrt(key_rows.shape[2])
    scores = (
        jnp.einsum("qhd,khd->hqk", query_block, key_rows, preferred_element_type=jnp.float32)
        * score_scale
    )
    allowed = (segment_block[:, None] == segment[None, :])[None]
    return jnp.where(allowed, scores, MASK_FILL)


def attend_forward(query_rows, key_rows, value_rows, segment):
    row_count = query_rows.shape[0]
    block_rows = min(512, row_count)

    def attend_block(block_index):
        block_start = block_index * block_rows
        query_block = lax.dynamic_slice_in_dim(query_rows, block_start, block_rows, 0)
        segment_block = lax.dynamic_slice_in_dim(segment, block_start, block_rows, 0)
        scores = block_scores(query_block, key_rows, segment_block, segment)
        row_max = jnp.max(scores, axis=2, keepdims=True)
        raised = jnp.exp(scores - row_max)
        row_total = jnp.sum(raised, axis=2, keepdims=True)
        weights = (raised / row_total).astype(jnp.bfloat16)
        mixed = jnp.einsum("hqk,khd->qhd", weights, value_rows, preferred_element_type=jnp.float32)
        return (mixed, (row_max + jnp.log(row_total))[:, :, 0])

    mixed_all, log_totals = lax.map(attend_block, jnp.arange(row_count // block_rows))
    return (mixed_all.reshape(query_rows.shape), log_totals)


def attend_backward(query_rows, key_rows, value_rows, segment, mixed_grad, log_totals):
    row_count = query_rows.shape[0]
    block_rows = min(512, row_count)
    score_scale = 1.0 / math.sqrt(key_rows.shape[2])
    zeros_kv = jnp.zeros(key_rows.shape, jnp.float32)

    def back_block(running, inputs):
        block_index, lse_block = inputs
        key_acc, value_acc = running
        block_start = block_index * block_rows
        query_block = lax.dynamic_slice_in_dim(query_rows, block_start, block_rows, 0)
        segment_block = lax.dynamic_slice_in_dim(segment, block_start, block_rows, 0)
        grad_block = lax.dynamic_slice_in_dim(mixed_grad, block_start, block_rows, 0)
        scores = block_scores(query_block, key_rows, segment_block, segment)
        weights = jnp.exp(scores - lse_block[:, :, None])
        weight_grad = jnp.einsum(
            "qhd,khd->hqk", grad_block, value_rows, preferred_element_type=jnp.float32
        )
        centre = jnp.sum(weights * weight_grad, axis=2, keepdims=True)
        score_grad = (weights * (weight_grad - centre)).astype(jnp.bfloat16)
        query_grad = (
            jnp.einsum("hqk,khd->qhd", score_grad, key_rows, preferred_element_type=jnp.float32)
            * score_scale
        )
        key_acc = (
            key_acc
            + jnp.einsum(
                "hqk,qhd->khd", score_grad, query_block, preferred_element_type=jnp.float32
            )
            * score_scale
        )
        value_acc = value_acc + jnp.einsum(
            "hqk,qhd->khd",
            weights.astype(jnp.bfloat16),
            grad_block,
            preferred_element_type=jnp.float32,
        )
        return ((key_acc, value_acc), query_grad)

    block_list = jnp.arange(row_count // block_rows)
    (key_grad, value_grad), query_grad = lax.scan(
        back_block, (zeros_kv, zeros_kv), (block_list, log_totals)
    )
    return (query_grad.reshape(query_rows.shape), key_grad, value_grad)


def run_forward(hidden_in, segment, visible, params, second_pass):
    (
        ln1_gain,
        ln1_shift,
        w_qkv,
        b_qv,
        w_out,
        b_out,
        ln2_gain,
        ln2_shift,
        w_fc1,
        b_fc1,
        w_fc2,
        b_fc2,
    ) = params
    row_count = hidden_in.shape[0]
    heads_here = w_out.shape[0] // HEAD_DIM
    head_shape = (row_count, heads_here, HEAD_DIM)
    normed_one = layer_norm(
        hidden_in, ln1_gain.astype(jnp.float32), ln1_shift.astype(jnp.float32)
    ).astype(jnp.bfloat16)
    projected = jnp.einsum("td,dcj->tcj", normed_one, w_qkv, preferred_element_type=jnp.float32)
    query_rows = (
        (projected[:, 0] + b_qv[0].astype(jnp.float32)).astype(jnp.bfloat16).reshape(head_shape)
    )
    key_rows = projected[:, 1].astype(jnp.bfloat16).reshape(head_shape)
    value_rows = (
        (projected[:, 2] + b_qv[1].astype(jnp.float32)).astype(jnp.bfloat16).reshape(head_shape)
    )
    mixed, log_totals = attend_forward(query_rows, key_rows, value_rows, segment)
    mixed_low = mixed.reshape(row_count, -1).astype(jnp.bfloat16)
    attn_part = jnp.dot(mixed_low, w_out, preferred_element_type=jnp.float32).astype(jnp.bfloat16)
    if second_pass:
        attn_total = lax.psum(attn_part, "tensor").astype(jnp.float32)
    else:
        attn_total = lax.psum(attn_part, "tensor").astype(jnp.float32)
    middle = hidden_in + attn_total + b_out.astype(jnp.float32)
    normed_two = layer_norm(
        middle, ln2_gain.astype(jnp.float32), ln2_shift.astype(jnp.float32)
    ).astype(jnp.bfloat16)
    hidden_pre = jnp.dot(normed_two, w_fc1, preferred_element_type=jnp.float32) + b_fc1.astype(
        jnp.float32
    )
    activated = jax.nn.gelu(hidden_pre, approximate=False).astype(jnp.bfloat16)
    kept_state = (
        normed_one,
        query_rows,
        key_rows,
        value_rows,
        log_totals,
        mixed_low,
        middle,
        normed_two,
        hidden_pre,
        activated,
    )
    if second_pass:
        return (None, kept_state)
    mlp_part = jnp.dot(activated, w_fc2, preferred_element_type=jnp.float32).astype(jnp.bfloat16)
    mlp_total = lax.psum(mlp_part, "tensor").astype(jnp.float32)
    result = jnp.where(visible[:, None], middle + mlp_total + b_fc2.astype(jnp.float32), 0.0)
    return (result, kept_state)


def sum_gradients(grads):
    large = [g.ndim == 2 and g.shape[0] > 2 or g.ndim == 3 for g in grads]
    low = lax.psum([g.astype(jnp.bfloat16) for g, w in zip(grads, large) if w], "dp")
    wide = lax.psum([g for g, w in zip(grads, large) if not w], "dp")
    return [low.pop(0).astype(jnp.float32) if w else wide.pop(0) for w in large]


def on_device(
    layer_input,
    patch_coords,
    item_lengths,
    out_grad,
    ln1_gain,
    ln1_shift,
    w_qkv,
    b_qv,
    w_out,
    b_out,
    ln2_gain,
    ln2_shift,
    w_fc1,
    b_fc1,
    w_fc2,
    b_fc2,
):
    segment_rows, visible_rows = item_layout(
        item_lengths.reshape(1, -1), layer_input.shape[0], item_lengths.shape[0]
    )
    segment = segment_rows[0]
    visible = visible_rows[0]
    hidden_in = layer_input.astype(jnp.float32) + sincos_table(patch_coords, layer_input.shape[1])
    params = (
        ln1_gain,
        ln1_shift,
        w_qkv,
        b_qv,
        w_out,
        b_out,
        ln2_gain,
        ln2_shift,
        w_fc1,
        b_fc1,
        w_fc2,
        b_fc2,
    )
    result, kept_state = run_forward(hidden_in, segment, visible, params, False)
    (
        normed_one,
        query_rows,
        key_rows,
        value_rows,
        log_totals,
        mixed_low,
        middle,
        normed_two,
        hidden_pre,
        activated,
    ) = kept_state
    top_grad = jnp.where(visible[:, None], out_grad, jnp.zeros_like(out_grad))
    top_grad_wide = top_grad.astype(jnp.float32)
    grad_b_fc2 = jnp.sum(top_grad_wide, axis=0)
    grad_w_fc2 = jnp.einsum("tf,td->fd", activated, top_grad, preferred_element_type=jnp.float32)
    act_grad = jnp.einsum("td,fd->tf", top_grad, w_fc2, preferred_element_type=jnp.float32)
    gelu_value, gelu_back = jax.vjp(partial(jax.nn.gelu, approximate=False), hidden_pre)
    pre_grad = gelu_back(act_grad)[0].astype(jnp.bfloat16)
    grad_b_fc1 = jnp.sum(pre_grad.astype(jnp.float32), axis=0)
    grad_w_fc1 = jnp.einsum("td,tf->df", normed_two, pre_grad, preferred_element_type=jnp.float32)
    norm_grad_part = jnp.einsum("tf,df->td", pre_grad, w_fc1, preferred_element_type=jnp.float32)
    norm_grad_two = lax.psum(norm_grad_part.astype(jnp.bfloat16), "tensor").astype(jnp.float32)
    unused_two, norm_back_two = jax.vjp(
        layer_norm, middle, ln2_gain.astype(jnp.float32), ln2_shift.astype(jnp.float32)
    )
    middle_ln, grad_ln2_gain, grad_ln2_shift = norm_back_two(norm_grad_two)
    middle_grad = top_grad_wide + middle_ln
    grad_b_out = jnp.sum(middle_grad, axis=0)
    middle_low = middle_grad.astype(jnp.bfloat16)
    grad_w_out = jnp.einsum("tj,td->jd", mixed_low, middle_low, preferred_element_type=jnp.float32)
    mixed_grad = (
        jnp.einsum("td,jd->tj", middle_low, w_out, preferred_element_type=jnp.float32)
        .astype(jnp.bfloat16)
        .reshape(query_rows.shape)
    )
    query_grad, key_grad, value_grad = attend_backward(
        query_rows, key_rows, value_rows, segment, mixed_grad, log_totals
    )
    row_count = query_rows.shape[0]
    proj_grad = (
        jnp.stack([query_grad, key_grad, value_grad], axis=1)
        .astype(jnp.bfloat16)
        .reshape(row_count, 3, -1)
    )
    grad_b_qv = jnp.sum(proj_grad[:, 0::2].astype(jnp.float32), axis=0)
    grad_w_qkv = jnp.einsum(
        "td,tcj->dcj", normed_one, proj_grad, preferred_element_type=jnp.float32
    )
    norm_grad_first = jnp.einsum(
        "tcj,dcj->td", proj_grad, w_qkv, preferred_element_type=jnp.float32
    )
    norm_grad_one = lax.psum(norm_grad_first.astype(jnp.bfloat16), "tensor").astype(jnp.float32)
    unused_one, norm_back_one = jax.vjp(
        layer_norm, hidden_in, ln1_gain.astype(jnp.float32), ln1_shift.astype(jnp.float32)
    )
    input_ln, grad_ln1_gain, grad_ln1_shift = norm_back_one(norm_grad_one)
    input_grad = middle_grad + input_ln
    (
        grad_ln1_gain,
        grad_ln1_shift,
        grad_w_qkv,
        grad_b_qv,
        grad_w_out,
        grad_b_out,
        grad_ln2_gain,
        grad_ln2_shift,
        grad_w_fc1,
        grad_b_fc1,
        grad_w_fc2,
        grad_b_fc2,
    ) = sum_gradients(
        (
            grad_ln1_gain,
            grad_ln1_shift,
            grad_w_qkv,
            grad_b_qv,
            grad_w_out,
            grad_b_out,
            grad_ln2_gain,
            grad_ln2_shift,
            grad_w_fc1,
            grad_b_fc1,
            grad_w_fc2,
            grad_b_fc2,
        )
    )
    return (
        result.astype(jnp.bfloat16),
        input_grad,
        grad_ln1_gain,
        grad_ln1_shift,
        grad_w_qkv,
        grad_b_qv,
        grad_w_out,
        grad_b_out,
        grad_ln2_gain,
        grad_ln2_shift,
        grad_w_fc1,
        grad_b_fc1,
        grad_w_fc2,
        grad_b_fc2,
    )


def solution(mesh):
    placed = (
        P("dp", None),
        P(None, "dp"),
        P("dp"),
        P("dp", None),
        P(),
        P(),
        P(None, None, "tensor"),
        P(None, "tensor"),
        P("tensor", None),
        P(),
        P(),
        P(),
        P(None, "tensor"),
        P("tensor"),
        P("tensor", None),
        P(),
    )
    return jax.shard_map(
        on_device,
        mesh=mesh,
        in_specs=placed,
        out_specs=(
            P("dp", None),
            P("dp", None),
            P(),
            P(),
            P(None, None, "tensor"),
            P(None, "tensor"),
            P("tensor", None),
            P(),
            P(),
            P(),
            P(None, "tensor"),
            P("tensor"),
            P("tensor", None),
            P(),
        ),
        check_vma=False,
    )
```

```python
import functools

import jax
import jax.numpy as jnp
from jax import lax
from jax.experimental import pallas as pl
from jax.experimental.pallas import tpu as pltpu
from jax.sharding import PartitionSpec as P

HEAD_DIM = 64
NORM_EPS = 1e-06
MASK_FILL = -1e30
LOG2E = 1.4426950408889634
BLK = 128
COORDS = 64
f32 = jnp.float32
bf16 = jnp.bfloat16


def mm(a, b):
    return lax.dot_general(a, b, (((1,), (0,)), ((), ())), preferred_element_type=f32)


def mm_nt(a, b):
    return lax.dot_general(a, b, (((1,), (1,)), ((), ())), preferred_element_type=f32)


def mm_tn(a, b):
    return lax.dot_general(a, b, (((0,), (0,)), ((), ())), preferred_element_type=f32)


def norm_parts(v):
    width = v.shape[-1]
    mean = jnp.sum(v, axis=-1, keepdims=True) * (1.0 / width)
    centred = v - mean
    spread = jnp.sum(centred * centred, axis=-1, keepdims=True) * (1.0 / width)
    r = lax.rsqrt(spread + NORM_EPS)
    return centred * r, r


def norm_back(u, gain, x_hat, r):
    width = u.shape[-1]
    ug = u * gain
    m1 = jnp.sum(ug, axis=-1, keepdims=True) * (1.0 / width)
    m2 = jnp.sum(ug * x_hat, axis=-1, keepdims=True) * (1.0 / width)
    return r * (ug - m1 - x_hat * m2)


def gelu_pair(v):
    phi = 0.5 * (1.0 + lax.erf(v * 0.7071067811865476))
    dens = jnp.exp(-0.5 * v * v) * 0.3989422804014327
    return v * phi, phi + v * dens


class Sems:
    def __init__(self):
        self.count = 0
        self.ready_count = 0
        self.ready = None
        self.send = None
        self.recv = None

    def take(self, n=1):
        first = self.count
        self.count += n
        return first


def remote(sems, idx, src, dst, target):
    return pltpu.make_async_remote_copy(
        src_ref=src,
        dst_ref=dst,
        send_sem=sems.send.at[idx],
        recv_sem=sems.recv.at[idx],
        device_id=target,
        device_id_type=pl.DeviceIdType.MESH,
    )


class Gather:
    def __init__(self, sems, parts, view, t):
        self.sems, self.view, self.t = sems, view, t
        self.base = sems.take(3 * parts)
        self.parts = parts
        self.sib = t + 1 - 2 * lax.rem(t, 2)
        self.opp = lax.rem(t + 2, 4)

    def copy(self, kind, s, owner):
        ref = self.view(s, owner)
        target = {"tensor": self.opp if kind == 1 else self.sib}
        return remote(self.sems, self.base + kind * self.parts + s, ref, ref, target)

    def start(self, s):
        self.copy(1, s, self.t).start()
        self.copy(0, s, self.t).start()

    def forward(self, s):
        self.copy(1, s, self.opp).wait_recv()
        self.copy(2, s, self.opp).start()

    def finish(self, s):
        self.copy(0, s, self.sib).wait_recv()
        self.copy(2, s, lax.rem(self.sib + 2, 4)).wait_recv()
        self.copy(0, s, self.t).wait_send()
        self.copy(1, s, self.t).wait_send()
        self.copy(2, s, self.opp).wait_send()


class Scatter:
    def __init__(self, sems, parts, bufs, t):
        self.part, self.got_a, self.got_b = bufs
        self.sems = sems
        self.base = sems.take(2 * parts)
        self.parts = parts
        self.core = lax.rem(t, 2)
        self.chip = t // 2
        self.sib = t + 1 - 2 * lax.rem(t, 2)
        self.opp = lax.rem(t + 2, 4)

    def store(self, s, value):
        for o in range(4):
            self.part[s, o % 2, o // 2] = value[o * BLK : (o + 1) * BLK].astype(bf16)

    def copy_a(self, s):
        return remote(
            self.sems, self.base + s, self.part.at[s, 1 - self.core], self.got_a.at[s], {"tensor": self.sib}
        )

    def copy_b(self, s):
        return remote(
            self.sems,
            self.base + self.parts + s,
            self.part.at[s, self.core, 1 - self.chip],
            self.got_b.at[s],
            {"tensor": self.opp},
        )

    def start(self, s):
        self.copy_a(s).start()

    def across(self, s):
        self.copy_a(s).wait()
        other = 1 - self.chip
        self.part[s, self.core, other] = (
            self.part[s, self.core, other].astype(f32) + self.got_a[s, other].astype(f32)
        ).astype(bf16)
        self.copy_b(s).start()

    def finish(self, s):
        self.copy_b(s).wait()
        return (
            self.part[s, self.core, self.chip].astype(f32)
            + self.got_a[s, self.chip].astype(f32)
            + self.got_b[s].astype(f32)
        )


class Reduce:
    def __init__(self, sems, ref, got, rows, cols, halvings, order, dp, log_n):
        self.sems, self.ref, self.got, self.cols = sems, ref, got, cols
        rest = [b for b in range(log_n) if b not in order[:halvings]]
        self.bits = list(order[:halvings]) + rest
        self.halvings = halvings
        self.dp = dp
        self.base = sems.take(len(self.bits) + halvings)
        self.ready = sems.ready_count
        sems.ready_count += halvings
        self.low, self.size, self.spot = [0], [rows], []
        at = 0
        for j, b in enumerate(self.bits):
            side = lax.rem(dp // (1 << b), 2)
            if j < halvings:
                half = self.size[-1] // 2
                self.low.append(self.low[-1] + side * half)
                self.size.append(half)
            else:
                self.low.append(self.low[-1])
                self.size.append(self.size[-1])
            self.spot.append(at)
            at += self.size[-1]

    @staticmethod
    def got_rows(rows, halvings, log_n):
        return sum(rows >> (j + 1) for j in range(halvings)) + (log_n - halvings) * (rows >> halvings)

    def partner(self, j):
        step = 1 << self.bits[j]
        return {"dp": self.dp + step * (1 - 2 * lax.rem(self.dp // step, 2))}

    def at(self, ref, low, size):
        if not isinstance(low, int):
            low = pl.multiple_of(low, 16)
        return ref.at[pl.ds(low, size), pl.ds(0, self.cols)]

    def copy_in(self, j):
        size = self.size[j + 1]
        if j < self.halvings:
            other = self.low[j] + self.low[j] + size - self.low[j + 1]
        else:
            other = self.low[j]
        return remote(
            self.sems,
            self.base + j,
            self.at(self.ref, other, size),
            self.at(self.got, self.spot[j], size),
            self.partner(j),
        )

    def copy_back(self, j):
        here = self.at(self.ref, self.low[j + 1], self.size[j + 1])
        return remote(self.sems, self.base + len(self.bits) + j, here, here, self.partner(j))

    def copy_home(self, j):
        size = self.size[j + 1]
        other = self.low[j] + self.low[j] + size - self.low[j + 1]
        here = self.at(self.ref, other, size)
        return remote(self.sems, self.base + len(self.bits) + j, here, here, self.partner(j))

    def begin(self, j):
        self.copy_in(j).start()

    def add(self, j):
        self.copy_in(j).wait()
        if j < self.halvings:
            pl.semaphore_signal(
                self.sems.ready.at[self.ready + j],
                inc=1,
                device_id=self.partner(j),
                device_id_type=pl.DeviceIdType.MESH,
            )
        mine = self.at(self.ref, self.low[j + 1], self.size[j + 1])
        theirs = self.at(self.got, self.spot[j], self.size[j + 1])
        mine[...] = (mine[...].astype(f32) + theirs[...].astype(f32)).astype(bf16)

    def give(self, j):
        pl.semaphore_wait(self.sems.ready.at[self.ready + j], 1)
        self.copy_back(j).start()

    def take(self, j):
        self.copy_back(j).wait_send()
        self.copy_home(j).wait_recv()

    def steps(self):
        out = [lambda: self.begin(0)]
        n = len(self.bits)
        for j in range(n):

            def step(j=j):
                self.add(j)
                if j + 1 < n:
                    self.begin(j + 1)
                else:
                    self.give(self.halvings - 1)

            out.append(step)
        for j in reversed(range(self.halvings)):

            def back(j=j):
                self.take(j)
                if j > 0:
                    self.give(j - 1)

            out.append(back)
        return out


def layer_kernel(
    geo,
    lens,
    x_in,
    og_in,
    coords,
    w_qkv,
    w_out_in,
    w_fc1_in,
    w_fc2_in,
    vecs,
    table,
    out_layer,
    out_input,
    out_fc2,
    out_fc1,
    out_wout,
    out_qkv,
    out_small,
    x_mg,
    tg,
    n1,
    q_t,
    k_t,
    v_t,
    rows3,
    probs,
    mix,
    linv,
    w_out,
    w_fc1,
    w_fc2,
    mid_own,
    n2_oi,
    act_ol,
    pg_dq,
    part0,
    got_a0,
    got_b0,
    part1,
    got_a1,
    got_b1,
    mg_own,
    do_t,
    delta,
    acc,
    g_fc2,
    g_fc1,
    g_wout,
    g_qkv,
    r_fc2,
    r_fc1,
    r_wout,
    r_qkv,
    segk,
    tab3,
    small,
    small_got,
    fc1_sums,
    send,
    recv,
    ready,
    local,
):
    parts, log_n, heads = geo
    size = 4 * BLK
    dp = lax.axis_index("dp")
    t = lax.axis_index("tensor")
    sib = t + 1 - 2 * lax.rem(t, 2)
    opp = lax.rem(t + 2, 4)
    width = x_mg.shape[1]
    hd = heads * HEAD_DIM

    sems = Sems()
    sems.send, sems.recv, sems.ready = send, recv, ready

    def part_rows(s):
        return pl.ds(pl.multiple_of(s * size, size), size)

    def own_rows(s, owner):
        return pl.ds(pl.multiple_of(s * size + owner * BLK, BLK), BLK)

    def slot_rows(s, owner):
        return pl.ds(pl.multiple_of(owner * (parts * BLK) + s * BLK, BLK), BLK)

    ag_w = Gather(sems, 1, lambda s, o: w_out.at[pl.ds(pl.multiple_of(o * hd, hd), hd)], t)
    ag_mix = Gather(sems, parts, lambda s, o: mix.at[s, pl.ds(pl.multiple_of(o * hd, hd), hd)], t)
    ag_mg = Gather(sems, parts, lambda s, o: x_mg.at[own_rows(s, o)], t)
    ag_out = Gather(sems, parts, lambda s, o: act_ol.at[slot_rows(s, o)], t)
    ag_in = Gather(sems, parts, lambda s, o: n2_oi.at[slot_rows(s, o)], t)
    rs_n2 = Scatter(sems, parts, (part0, got_a0, got_b0), t)
    rs_mlp = Scatter(sems, parts, (part1, got_a1, got_b1), t)
    rs_n1 = Scatter(sems, parts, (part0, got_a0, got_b0), t)
    dp_fc2 = Reduce(sems, g_fc2, r_fc2, width, width, 3, (0, 1, 2), dp, log_n)
    dp_fc1 = Reduce(sems, g_fc1, r_fc1, width, width, 3, (0, 1, 2), dp, log_n)
    dp_wout = Reduce(sems, g_wout, r_wout, hd, width, 2, (1, 0), dp, log_n)
    dp_qkv = Reduce(sems, g_qkv, r_qkv, width, 3 * hd, 3, (0, 1, 2), dp, log_n)
    small_base = sems.take(2 + log_n)

    n_local = [0]
    pending = []

    def fetch(src, dst):
        cp = pltpu.make_async_copy(src, dst, local.at[n_local[0]])
        n_local[0] += 1
        cp.start()
        return cp

    x_loads = [
        [fetch(x_in.at[slot_rows(s, o)], x_mg.at[own_rows(s, o)]) for o in range(4)] for s in range(parts)
    ]
    w_out_load = fetch(w_out_in, w_out.at[pl.ds(pl.multiple_of(t * hd, hd), hd)])
    fc1_load = fetch(w_fc1_in, w_fc1)
    fc2_load = fetch(w_fc2_in, w_fc2)
    tg_loads = [
        fetch(og_in.at[slot_rows(s, o)], tg.at[own_rows(s, o)]) for s in range(parts) for o in range(4)
    ]

    barrier = pltpu.get_barrier_semaphore()
    for target in (sib, opp):
        pl.semaphore_signal(
            barrier, inc=1, device_id={"tensor": target}, device_id_type=pl.DeviceIdType.MESH
        )
    for b in range(log_n):
        step = 1 << b
        other = dp + step * (1 - 2 * lax.rem(dp // step, 2))
        pl.semaphore_signal(
            barrier, inc=1, device_id={"dp": other}, device_id_type=pl.DeviceIdType.MESH
        )
    pl.semaphore_wait(barrier, 2 + log_n)

    w_out_load.wait()
    ag_w.start(0)

    whole = table[...]
    hi = whole.astype(bf16)
    rest = whole - hi.astype(f32)
    mi = rest.astype(bf16)
    tab3[pl.ds(0, COORDS)] = hi
    tab3[pl.ds(COORDS, COORDS)] = mi
    tab3[pl.ds(2 * COORDS, COORDS)] = (rest - mi.astype(f32)).astype(bf16)

    ln1_gain, ln1_shift = vecs[0:1, :], vecs[1:2, :]
    ln2_gain, ln2_shift = vecs[2:3, :], vecs[3:4, :]
    b_out, b_fc2, b_fc1 = vecs[4:5, :], vecs[5:6, :], vecs[6:7, :]
    b_q, b_v = vecs[7:8, :hd], vecs[8:9, :hd]

    ends, total = [], 0
    for i in range(lens.shape[0]):
        total = total + lens[i]
        ends.append(total)

    def segment_of(place):
        passed = jnp.zeros_like(place)
        for e in ends:
            passed = passed + jnp.where(place >= e, 1, 0)
        return jnp.where(place < ends[-1], passed, len(ends) + place)

    def positions(rows_of, c):
        n = c.shape[1]
        values = lax.broadcasted_iota(jnp.int32, (COORDS, n), 0)
        cols = []
        for i in range(3):
            hot = jnp.where(values == c[i : i + 1, :], 1.0, 0.0).astype(bf16)
            cols.append(mm_tn(jnp.concatenate([hot, hot, hot], axis=0), tab3[...]))
        return jnp.concatenate(cols, axis=1)

    def lane_blocks(ref, s):
        return jnp.concatenate([ref[:, slot_rows(s, o)] for o in range(4)], axis=1)

    def hidden_of(s):
        return x_mg[part_rows(s), :].astype(f32) + positions(None, lane_blocks(coords, s))

    for s in range(parts):
        for cp in x_loads[s]:
            cp.wait()

    def project(s, carry):
        for o in range(4):
            place = lax.broadcasted_iota(jnp.int32, (BLK, BLK), 0) + (o * parts * BLK + s * BLK)
            segk[own_rows(s, o), :] = segment_of(place)
        x_hat, _ = norm_parts(hidden_of(s))
        low = (x_hat * ln1_gain + ln1_shift).astype(bf16)
        n1[part_rows(s), :] = low
        proj = mm(low, w_qkv[...])
        q = (proj[:, :hd] + b_q).astype(bf16).astype(f32).T.astype(bf16)
        k = proj[:, hd : 2 * hd].astype(bf16).astype(f32).T.astype(bf16)
        v = (proj[:, 2 * hd :] + b_v).astype(bf16).astype(f32).T.astype(bf16)
        for h in range(heads):
            head = slice(h * HEAD_DIM, (h + 1) * HEAD_DIM)
            q_t[h, :, part_rows(s)] = q[head]
            k_t[h, :, part_rows(s)] = k[head]
            v_t[h, :, part_rows(s)] = v[head]
            rows3[h, part_rows(s), :] = k[head].astype(f32).T.astype(bf16)
        return carry

    lax.fori_loop(0, parts, project, 0)

    def attend(s, carry):
        place = jnp.concatenate(
            [
                lax.broadcasted_iota(jnp.int32, (1, BLK), 1) + (o * parts * BLK + s * BLK)
                for o in range(4)
            ],
            axis=1,
        )
        allowed = segk[...][:, :1] == segment_of(place)
        for h in range(heads):
            scores = mm(rows3[h], q_t[h, :, part_rows(s)])
            scores = jnp.where(allowed, scores * (LOG2E / HEAD_DIM**0.5), MASK_FILL)
            top = jnp.max(scores, axis=0, keepdims=True)
            raised = jnp.exp2(scores - top)
            inv = 1.0 / jnp.sum(raised, axis=0, keepdims=True)
            low = raised.astype(bf16)
            probs[h, :, part_rows(s)] = low
            linv[h, :, part_rows(s)] = inv
            mixed = mm(v_t[h], low) * inv
            mix[s, pl.ds(pl.multiple_of(t * hd + h * HEAD_DIM, HEAD_DIM), HEAD_DIM), :] = mixed.astype(bf16)
        ag_mix.start(s)

        @pl.when(s >= 1)
        def _():
            ag_mix.forward(s - 1)

        return carry

    lax.fori_loop(0, parts, attend, 0)
    ag_w.forward(0)
    for cp in tg_loads:
        cp.wait()
    fc1_load.wait()
    fc2_load.wait()
    ag_w.finish(0)
    fc1_sums[...] = jnp.zeros_like(fc1_sums)
    small[0] = jnp.zeros_like(small[0])

    def visible_rows(s, owner):
        return segk[own_rows(s, owner), :][:, :1] < len(ends)

    def second_norm_back(s):
        u = rs_n2.finish(s)
        middle = mid_own[s]
        x_hat, r = norm_parts(middle)
        grad = tg[own_rows(s, t), :].astype(f32) + norm_back(u, ln2_gain, x_hat, r)
        mg_own[s] = grad
        small[0, 2:3, :] += jnp.sum(u * x_hat, axis=0, keepdims=True)
        small[0, 3:4, :] += jnp.sum(u, axis=0, keepdims=True)
        small[0, 4:5, :] += jnp.sum(grad, axis=0, keepdims=True)
        small[0, 5:6, :] += jnp.sum(tg[own_rows(s, t), :].astype(f32), axis=0, keepdims=True)
        x_mg[own_rows(s, t), :] = grad.astype(bf16)
        ag_mg.start(s)

    def feed(s, carry):
        @pl.when(s == parts - 1)
        def _():
            ag_mix.forward(s)

        ag_mix.finish(s)
        attn = mm_tn(mix[s], w_out[...])
        middle = hidden_of(s) + attn + b_out
        mine = middle[:BLK]
        for o in range(1, 4):
            mine = jnp.where(t == o, middle[o * BLK : (o + 1) * BLK], mine)
        mid_own[s] = mine
        x_hat, _ = norm_parts(middle)
        low = (x_hat * ln2_gain + ln2_shift).astype(bf16)
        n2_oi[part_rows(s), :] = low
        value, slope = gelu_pair(mm(low, w_fc1[...]) + b_fc1)
        act_ol[part_rows(s), :] = value.astype(bf16)
        shown = segk[part_rows(s), :][:, :1] < len(ends)
        top = jnp.where(shown, tg[part_rows(s), :].astype(f32), 0.0).astype(bf16)
        tg[part_rows(s), :] = top
        pre = (mm_nt(top, w_fc2[...]) * slope).astype(bf16)
        pg_dq[part_rows(s), :] = pre
        fc1_sums[0:1, :] += jnp.sum(pre.astype(f32), axis=0, keepdims=True)
        rs_n2.store(s, mm_nt(pre, w_fc1[...]))
        rs_n2.start(s)

        @pl.when(s >= 1)
        def _():
            second_norm_back(s - 1)

        @pl.when(s >= 2)
        def _():
            ag_mg.forward(s - 2)

        rs_mlp.store(s, mm(act_ol[part_rows(s), :], w_fc2[...]))
        rs_n2.across(s)
        return carry

    lax.fori_loop(0, parts, feed, 0)

    def weight_grad(dst, left, right, cols):
        for i in range(left.shape[1] // 256):
            dst[i * 256 : (i + 1) * 256, :cols] = mm_tn(left[:, i * 256 : (i + 1) * 256], right[:, :cols]).astype(bf16)

    s_fc2, s_fc1, s_wout, s_qkv = dp_fc2.steps(), dp_fc1.steps(), dp_wout.steps(), dp_qkv.steps()

    def go(steps, n=1):
        for _ in range(n):
            if steps:
                steps.pop(0)()

    weight_grad(g_fc2, act_ol, tg, width)
    go(s_fc2)
    second_norm_back(parts - 1)
    x_own_loads = [fetch(x_in.at[slot_rows(s, t)], tg.at[own_rows(s, t)]) for s in range(parts)]
    if parts >= 2:
        ag_mg.forward(parts - 2)
    weight_grad(g_fc1, n2_oi, pg_dq, width)
    go(s_fc1)
    ag_mg.forward(parts - 1)
    for s in range(parts):
        ag_mg.finish(s)
    for s in range(parts):
        rs_mlp.start(s)

    for s in range(parts):
        rows = part_rows(s)
        own = pl.ds(pl.multiple_of(t * hd, hd), hd)
        low = mm_nt(x_mg[rows, :], w_out[own, :]).astype(bf16).astype(f32).T
        for h in range(heads):
            scaled = (low[h * HEAD_DIM : (h + 1) * HEAD_DIM] * linv[h, :, rows]).astype(bf16)
            do_t[h, :, rows] = scaled
            mixed = mix[s, pl.ds(pl.multiple_of(t * hd + h * HEAD_DIM, HEAD_DIM), HEAD_DIM), :]
            delta[h, :, rows] = jnp.sum(scaled.astype(f32) * mixed.astype(f32), axis=0, keepdims=True)
    for s in range(parts):
        rs_mlp.across(s)
    own = pl.ds(pl.multiple_of(t * hd, hd), hd)
    grad_out = mm(mix[0, own, :], x_mg[part_rows(0), :])
    for s in range(1, parts):
        grad_out = grad_out + mm(mix[s, own, :], x_mg[part_rows(s), :])
    g_wout[...] = grad_out.astype(bf16)
    go(s_wout)

    for h in range(heads):
        rows3[0] = v_t[h].astype(f32).T.astype(bf16)
        rows3[1] = q_t[h].astype(f32).T.astype(bf16)
        rows3[2] = do_t[h].astype(f32).T.astype(bf16)

        def back(s, carry, h=h):
            rows = part_rows(s)
            p = probs[h, rows, :]
            wg = mm(rows3[0, rows, :], do_t[h])
            sg = (p.astype(f32) * (wg - delta[h])).astype(bf16)
            dv = mm(p, rows3[2])
            dk = mm(sg, rows3[1]) * (1.0 / HEAD_DIM**0.5)
            pg_dq[rows, hd + h * HEAD_DIM : hd + (h + 1) * HEAD_DIM] = dk.astype(bf16)
            pg_dq[rows, 2 * hd + h * HEAD_DIM : 2 * hd + (h + 1) * HEAD_DIM] = dv.astype(bf16)
            dq = mm(k_t[h, :, rows], sg)

            @pl.when(s == 0)
            def _():
                acc[...] = dq

            @pl.when(s > 0)
            def _():
                acc[...] += dq

            return carry

        lax.fori_loop(0, parts, back, 0)
        pg_dq[:, h * HEAD_DIM : (h + 1) * HEAD_DIM] = (acc[...].T * (1.0 / HEAD_DIM**0.5)).astype(bf16)
        go(s_fc2)
        go(s_fc1)
        if h == 1:
            go(s_wout)

    for s in range(parts):
        rs_n1.store(s, mm_nt(pg_dq[part_rows(s), : 3 * hd], w_qkv[...]))
        rs_n1.start(s)
        if s >= 1:
            rs_n1.across(s - 1)
    weight_grad(g_qkv, n1, pg_dq, 3 * hd)
    rs_n1.across(parts - 1)
    go(s_qkv)
    sums = jnp.sum(pg_dq[:, : 3 * hd].astype(f32), axis=0, keepdims=True)
    small[0, 8:9, :] = fc1_sums[0:1, :]
    small[0, 9:10, :hd] = sums[:, :hd]
    small[0, 10:11, :hd] = sums[:, 2 * hd :]

    def first_norm_back(s):
        u = rs_n1.finish(s)
        hidden = tg[own_rows(s, t), :].astype(f32) + positions(None, coords[:, slot_rows(s, t)])
        x_hat, r = norm_parts(hidden)
        grad = mg_own[s] + norm_back(u, ln1_gain, x_hat, r)
        small[0, 0:1, :] += jnp.sum(u * x_hat, axis=0, keepdims=True)
        small[0, 1:2, :] += jnp.sum(u, axis=0, keepdims=True)
        n2_oi[slot_rows(s, t), :] = grad.astype(bf16)
        ag_in.start(s)

    for cp in x_own_loads:
        cp.wait()
    for s in range(parts):
        first_norm_back(s)
        if s >= 1:
            ag_in.forward(s - 1)
        go(s_fc2)
        go(s_fc1)
        go(s_wout)
        go(s_qkv)

    def layer_out(s):
        total = mid_own[s] + rs_mlp.finish(s) + b_fc2
        act_ol[slot_rows(s, t), :] = jnp.where(visible_rows(s, t), total, 0.0).astype(bf16)
        ag_out.start(s)

    for s in range(parts):
        layer_out(s)
    ag_in.forward(parts - 1)

    def small_copy(i, rows, target):
        return remote(
            sems, small_base + i, small.at[i, pl.ds(0, rows)], small_got.at[i, pl.ds(0, rows)], target
        )

    hops = [(8, {"tensor": sib}), (8, {"tensor": opp})]
    for b in range(log_n):
        step = 1 << b
        hops.append((16, {"dp": dp + step * (1 - 2 * lax.rem(dp // step, 2))}))
    for i, (rows, target) in enumerate(hops):
        cp = small_copy(i, rows, target)
        cp.start()
        cp.wait()
        small[i + 1, 0:rows] = small[i, 0:rows] + small_got[i, 0:rows]
        if rows < 16:
            small[i + 1, rows:16] = small[i, rows:16]
        go(s_qkv)
        go(s_fc2)
        go(s_fc1)
        go(s_wout)

    outs = []
    for steps, ref, dst in (
        (s_fc2, g_fc2, out_fc2),
        (s_fc1, g_fc1, out_fc1),
        (s_wout, g_wout, out_wout),
    ):
        go(steps, len(steps))
        outs.append(fetch(ref, dst))
    outs.append(fetch(small.at[len(hops)], out_small))
    for s in range(parts):
        ag_in.finish(s)
    outs.append(fetch(n2_oi, out_input))
    for s in range(parts):
        ag_out.forward(s)
    for s in range(parts):
        ag_out.finish(s)
    outs.append(fetch(act_ol, out_layer))
    go(s_qkv, len(s_qkv))
    outs.append(fetch(g_qkv, out_qkv))
    for cp in outs:
        cp.wait()


def sincos_rows(feature_count):
    half_width = feature_count // 6
    ladder = jnp.arange(half_width, dtype=f32) / half_width
    frequency = jnp.power(10000.0, -ladder)
    angles = jnp.arange(COORDS, dtype=jnp.int32).astype(f32)[:, None] * frequency[None, :]
    return jnp.concatenate([jnp.sin(angles), jnp.cos(angles)], axis=1)


def on_device(
    n_dp,
    layer_input,
    patch_coords,
    item_lengths,
    out_grad,
    ln1_gain,
    ln1_shift,
    w_qkv,
    b_qv,
    w_out,
    b_out,
    ln2_gain,
    ln2_shift,
    w_fc1,
    b_fc1,
    w_fc2,
    b_fc2,
):
    tokens, width = layer_input.shape
    hd = w_out.shape[0]
    ff = w_fc1.shape[1]
    heads = hd // HEAD_DIM
    parts = tokens // (4 * BLK)
    log_n = n_dp.bit_length() - 1
    size = 4 * BLK
    pad = lambda v: jnp.pad(v, (0, width - v.shape[0]))
    vecs = jnp.stack(
        [
            pad(v.astype(f32))
            for v in (ln1_gain, ln1_shift, ln2_gain, ln2_shift, b_out, b_fc2, b_fc1, b_qv[0], b_qv[1])
        ]
        + [jnp.zeros((width,), f32)] * 7
    )
    got = Reduce.got_rows
    vmem = lambda *s: pltpu.VMEM(s, bf16)
    vmem32 = lambda *s: pltpu.VMEM(s, f32)
    scratch = [
        vmem(tokens, width),
        vmem(tokens, width),
        vmem(tokens, width),
        vmem(heads, HEAD_DIM, tokens),
        vmem(heads, HEAD_DIM, tokens),
        vmem(heads, HEAD_DIM, tokens),
        vmem(heads, tokens, HEAD_DIM),
        vmem(heads, tokens, tokens),
        vmem(parts, 4 * hd, size),
        vmem32(heads, 1, tokens),
        vmem(4 * hd, width),
        vmem(width, ff),
        vmem(ff, width),
        vmem32(parts, BLK, width),
        vmem(tokens, width),
        vmem(tokens, width),
        vmem(tokens, width),
    ]
    for _ in range(2):
        scratch += [
            vmem(parts, 2, 2, BLK, width),
            vmem(parts, 2, BLK, width),
            vmem(parts, BLK, width),
        ]
    scratch += [
        vmem32(parts, BLK, width),
        vmem(heads, HEAD_DIM, tokens),
        vmem32(heads, 1, tokens),
        vmem32(HEAD_DIM, tokens),
        vmem(ff, width),
        vmem(width, ff),
        vmem(hd, width),
        vmem(width, 3 * hd),
        vmem(got(ff, 3, log_n), width),
        vmem(got(width, 3, log_n), width),
        vmem(got(hd, 2, log_n), width),
        vmem(got(width, 3, log_n), 3 * hd),
        pltpu.VMEM((tokens, BLK), jnp.int32),
        vmem(3 * COORDS, 2 * (width // 6)),
        vmem32(3 + log_n, 16, width),
        vmem32(2 + log_n, 16, width),
        vmem32(8, ff),
    ]
    n_sems = 3 + 4 * 3 * parts + 3 * 2 * parts + 3 * (log_n + 3) + (log_n + 2) + 2 + log_n
    scratch += [
        pltpu.SemaphoreType.DMA((n_sems,)),
        pltpu.SemaphoreType.DMA((n_sems,)),
        pltpu.SemaphoreType.REGULAR((11,)),
        pltpu.SemaphoreType.DMA((4 * parts * 2 + parts + 3 + 7,)),
    ]
    shape = jax.ShapeDtypeStruct
    hbm = pl.BlockSpec(memory_space=pl.ANY)
    here = pl.BlockSpec(memory_space=pltpu.VMEM)
    results = pl.pallas_call(
        functools.partial(layer_kernel, (parts, log_n, heads)),
        name="layer",
        out_shape=(
            shape((tokens, width), bf16),
            shape((tokens, width), bf16),
            shape((ff, width), bf16),
            shape((width, ff), bf16),
            shape((hd, width), bf16),
            shape((width, 3 * hd), bf16),
            shape((16, width), f32),
        ),
        in_specs=[pl.BlockSpec(memory_space=pltpu.SMEM), hbm, hbm, here, here, hbm, hbm, hbm, here, here],
        out_specs=(hbm,) * 7,
        scratch_shapes=scratch,
        compiler_params=pltpu.CompilerParams(
            collective_id=0, has_side_effects=True, vmem_limit_bytes=67043328
        ),
    )(
        item_lengths,
        layer_input,
        out_grad,
        patch_coords,
        w_qkv.reshape(width, 3 * hd),
        w_out,
        w_fc1,
        w_fc2,
        vecs,
        sincos_rows(width),
    )
    layer_output, input_grad, g_fc2, g_fc1, g_wout, g_qkv, small = results
    return (
        layer_output,
        input_grad.astype(f32),
        small[0],
        small[1],
        g_qkv.astype(f32).reshape(width, 3, hd),
        small[9:11, :hd],
        g_wout.astype(f32),
        small[4],
        small[2],
        small[3],
        g_fc1.astype(f32),
        small[8, :ff],
        g_fc2.astype(f32),
        small[5],
    )


def solution(mesh):
    placed = (
        P("dp", None),
        P(None, "dp"),
        P("dp"),
        P("dp", None),
        P(),
        P(),
        P(None, None, "tensor"),
        P(None, "tensor"),
        P("tensor", None),
        P(),
        P(),
        P(),
        P(None, "tensor"),
        P("tensor"),
        P("tensor", None),
        P(),
    )
    return jax.shard_map(
        functools.partial(on_device, mesh.shape["dp"]),
        mesh=mesh,
        in_specs=placed,
        out_specs=(
            P("dp", None),
            P("dp", None),
            P(),
            P(),
            P(None, None, "tensor"),
            P(None, "tensor"),
            P("tensor", None),
            P(),
            P(),
            P(),
            P(None, "tensor"),
            P("tensor"),
            P("tensor", None),
            P(),
        ),
        check_vma=False,
    )
```

```python
import functools

import jax
import jax.numpy as jnp
import ml_dtypes
import numpy as np
from jax import lax
from jax.experimental import pallas as pl
from jax.experimental.pallas import tpu as pltpu
from jax.sharding import PartitionSpec as P

HEAD_DIM = 64
NORM_EPS = 1e-06
MASK_FILL = -1e30
LOG2E = 1.4426950408889634
BLK = 128
COORDS = 64
f32 = jnp.float32
bf16 = jnp.bfloat16


def mm(a, b):
    return lax.dot_general(a, b, (((1,), (0,)), ((), ())), preferred_element_type=f32)


def mm_nt(a, b):
    return lax.dot_general(a, b, (((1,), (1,)), ((), ())), preferred_element_type=f32)


def mm_tn(a, b):
    return lax.dot_general(a, b, (((0,), (0,)), ((), ())), preferred_element_type=f32)


def norm_parts(v):
    width = v.shape[-1]
    mean = jnp.sum(v, axis=-1, keepdims=True) * (1.0 / width)
    centred = v - mean
    spread = jnp.sum(centred * centred, axis=-1, keepdims=True) * (1.0 / width)
    r = lax.rsqrt(spread + NORM_EPS)
    return centred * r, r


def norm_back(u, gain, x_hat, r):
    width = u.shape[-1]
    ug = u * gain
    m1 = jnp.sum(ug, axis=-1, keepdims=True) * (1.0 / width)
    m2 = jnp.sum(ug * x_hat, axis=-1, keepdims=True) * (1.0 / width)
    return r * (ug - m1 - x_hat * m2)


def gelu_pair(v):
    phi = 0.5 * (1.0 + lax.erf(v * 0.7071067811865476))
    dens = jnp.exp(-0.5 * v * v) * 0.3989422804014327
    return v * phi, phi + v * dens


class Sems:
    def __init__(self):
        self.count = 0
        self.ready_count = 0
        self.ready = None
        self.send = None
        self.recv = None

    def take(self, n=1):
        first = self.count
        self.count += n
        return first


def remote(sems, idx, src, dst, target):
    return pltpu.make_async_remote_copy(
        src_ref=src,
        dst_ref=dst,
        send_sem=sems.send.at[idx],
        recv_sem=sems.recv.at[idx],
        device_id=target,
        device_id_type=pl.DeviceIdType.MESH,
    )


class Gather:
    def __init__(self, sems, parts, view, t):
        self.sems, self.view, self.t = sems, view, t
        self.base = sems.take(3 * parts)
        self.parts = parts
        self.sib = t + 1 - 2 * lax.rem(t, 2)
        self.opp = lax.rem(t + 2, 4)

    def copy(self, kind, s, owner):
        ref = self.view(s, owner)
        target = {"tensor": self.opp if kind == 1 else self.sib}
        return remote(self.sems, self.base + kind * self.parts + s, ref, ref, target)

    def start(self, s):
        self.copy(1, s, self.t).start()
        self.copy(0, s, self.t).start()

    def forward(self, s):
        self.copy(1, s, self.opp).wait_recv()
        self.copy(2, s, self.opp).start()

    def finish(self, s):
        self.copy(0, s, self.sib).wait_recv()
        self.copy(2, s, lax.rem(self.sib + 2, 4)).wait_recv()
        self.copy(0, s, self.t).wait_send()
        self.copy(1, s, self.t).wait_send()
        self.copy(2, s, self.opp).wait_send()


class Scatter:
    def __init__(self, sems, parts, bufs, t):
        self.part, self.got_a, self.got_b = bufs
        self.sems = sems
        self.base = sems.take(2 * parts)
        self.parts = parts
        self.core = lax.rem(t, 2)
        self.chip = t // 2
        self.sib = t + 1 - 2 * lax.rem(t, 2)
        self.opp = lax.rem(t + 2, 4)

    def store(self, s, value):
        for o in range(4):
            self.part[s, o % 2, o // 2] = value[o * BLK : (o + 1) * BLK].astype(bf16)

    def copy_a(self, s):
        return remote(
            self.sems, self.base + s, self.part.at[s, 1 - self.core], self.got_a.at[s], {"tensor": self.sib}
        )

    def copy_b(self, s):
        return remote(
            self.sems,
            self.base + self.parts + s,
            self.part.at[s, self.core, 1 - self.chip],
            self.got_b.at[s],
            {"tensor": self.opp},
        )

    def start(self, s):
        self.copy_a(s).start()

    def across(self, s):
        self.copy_a(s).wait()
        other = 1 - self.chip
        self.part[s, self.core, other] = (
            self.part[s, self.core, other].astype(f32) + self.got_a[s, other].astype(f32)
        ).astype(bf16)
        self.copy_b(s).start()

    def finish(self, s):
        self.copy_b(s).wait()
        return (
            self.part[s, self.core, self.chip].astype(f32)
            + self.got_a[s, self.chip].astype(f32)
            + self.got_b[s].astype(f32)
        )


class Reduce:
    def __init__(self, sems, ref, got, rows, cols, halvings, order, dp, log_n, first=0):
        self.sems, self.ref, self.got, self.cols = sems, ref, got, cols
        rest = [b for b in range(log_n) if b not in order[:halvings]]
        self.bits = list(order[:halvings]) + rest
        self.halvings = halvings
        self.dp = dp
        self.base = sems.take(len(self.bits) + halvings)
        self.ready = sems.ready_count
        sems.ready_count += halvings
        self.low, self.size, self.spot = [first], [rows], []
        at = 0
        for j, b in enumerate(self.bits):
            side = lax.rem(dp // (1 << b), 2)
            if j < halvings:
                half = self.size[-1] // 2
                self.low.append(self.low[-1] + side * half)
                self.size.append(half)
            else:
                self.low.append(self.low[-1])
                self.size.append(self.size[-1])
            self.spot.append(at)
            at += self.size[-1]

    @staticmethod
    def got_rows(rows, halvings, log_n):
        return sum(rows >> (j + 1) for j in range(halvings)) + (log_n - halvings) * (rows >> halvings)

    def partner(self, j):
        step = 1 << self.bits[j]
        return {"dp": self.dp + step * (1 - 2 * lax.rem(self.dp // step, 2))}

    def at(self, ref, low, size):
        if not isinstance(low, int):
            low = pl.multiple_of(low, 16)
        return ref.at[pl.ds(low, size), pl.ds(0, self.cols)]

    def copy_in(self, j):
        size = self.size[j + 1]
        if j < self.halvings:
            other = self.low[j] + self.low[j] + size - self.low[j + 1]
        else:
            other = self.low[j]
        return remote(
            self.sems,
            self.base + j,
            self.at(self.ref, other, size),
            self.at(self.got, self.spot[j], size),
            self.partner(j),
        )

    def copy_back(self, j):
        here = self.at(self.ref, self.low[j + 1], self.size[j + 1])
        return remote(self.sems, self.base + len(self.bits) + j, here, here, self.partner(j))

    def copy_home(self, j):
        size = self.size[j + 1]
        other = self.low[j] + self.low[j] + size - self.low[j + 1]
        here = self.at(self.ref, other, size)
        return remote(self.sems, self.base + len(self.bits) + j, here, here, self.partner(j))

    def begin(self, j):
        self.copy_in(j).start()

    def add(self, j):
        self.copy_in(j).wait()
        if j < self.halvings:
            pl.semaphore_signal(
                self.sems.ready.at[self.ready + j],
                inc=1,
                device_id=self.partner(j),
                device_id_type=pl.DeviceIdType.MESH,
            )
        mine = self.at(self.ref, self.low[j + 1], self.size[j + 1])
        theirs = self.at(self.got, self.spot[j], self.size[j + 1])
        mine[...] = (mine[...].astype(f32) + theirs[...].astype(f32)).astype(bf16)

    def give(self, j):
        pl.semaphore_wait(self.sems.ready.at[self.ready + j], 1)
        self.copy_back(j).start()

    def take(self, j):
        self.copy_back(j).wait_send()
        self.copy_home(j).wait_recv()

    def steps(self):
        out = [lambda: self.begin(0)]
        n = len(self.bits)
        for j in range(n):

            def step(j=j):
                self.add(j)
                if j + 1 < n:
                    self.begin(j + 1)
                else:
                    self.give(self.halvings - 1)

            out.append(step)
        for j in reversed(range(self.halvings)):

            def back(j=j):
                self.take(j)
                if j > 0:
                    self.give(j - 1)

            out.append(back)
        return out


def layer_kernel(
    geo,
    lens,
    x_in,
    og_in,
    coords,
    w_qkv,
    w_out_in,
    w_fc1_in,
    w_fc2_in,
    v0,
    v1,
    v2,
    v3,
    v4,
    v5,
    v6,
    b_qv,
    tab3,
    out_layer,
    out_input,
    out_fc2,
    out_fc1,
    out_wout,
    out_qkv,
    out_small,
    x_mg,
    tg,
    n1,
    q_t,
    k_t,
    v_t,
    rows3,
    probs,
    mix,
    linv,
    w_out,
    w_fc1,
    w_fc2,
    mid_own,
    n2_oi,
    act_ol,
    pg_dq,
    part0,
    got_a0,
    got_b0,
    part1,
    got_a1,
    got_b1,
    mg_own,
    do_t,
    delta,
    acc,
    g_fc2,
    g_fc1,
    g_wout,
    g_qkv,
    r_fc2,
    r_fc1,
    r_wout,
    r_qa,
    r_qb,
    segk,
    small,
    small_got,
    fc1_sums,
    send,
    recv,
    ready,
    local,
):
    parts, log_n, heads = geo
    vecs = (v0, v1, v2, v3, v4, v5, v6)
    size = 4 * BLK
    dp = lax.axis_index("dp")
    t = lax.axis_index("tensor")
    sib = t + 1 - 2 * lax.rem(t, 2)
    opp = lax.rem(t + 2, 4)
    width = x_mg.shape[1]
    hd = heads * HEAD_DIM

    sems = Sems()
    sems.send, sems.recv, sems.ready = send, recv, ready

    def part_rows(s):
        return pl.ds(pl.multiple_of(s * size, size), size)

    def own_rows(s, owner):
        return pl.ds(pl.multiple_of(s * size + owner * BLK, BLK), BLK)

    def slot_rows(s, owner):
        return pl.ds(pl.multiple_of(owner * (parts * BLK) + s * BLK, BLK), BLK)

    ag_w = Gather(sems, 1, lambda s, o: w_out.at[pl.ds(pl.multiple_of(o * hd, hd), hd)], t)
    ag_mix = Gather(sems, parts, lambda s, o: mix.at[s, pl.ds(pl.multiple_of(o * hd, hd), hd)], t)
    ag_mg = Gather(sems, parts, lambda s, o: x_mg.at[own_rows(s, o)], t)
    ag_out = Gather(sems, parts, lambda s, o: act_ol.at[slot_rows(s, o)], t)
    ag_in = Gather(sems, parts, lambda s, o: n2_oi.at[slot_rows(s, o)], t)
    rs_n2 = Scatter(sems, parts, (part0, got_a0, got_b0), t)
    rs_mlp = Scatter(sems, parts, (part1, got_a1, got_b1), t)
    rs_n1 = Scatter(sems, parts, (part0, got_a0, got_b0), t)
    dp_fc2 = Reduce(sems, g_fc2, r_fc2, width, width, 3, (0, 1, 2), dp, log_n)
    dp_fc1 = Reduce(sems, g_fc1, r_fc1, width, width, 3, (1, 0, 2), dp, log_n)
    dp_wout = Reduce(sems, g_wout, r_wout, hd, width, 2, (1, 0), dp, log_n)
    half = width // 2
    dp_qa = Reduce(sems, g_qkv, r_qa, half, 3 * hd, 3, (0, 1, 2), dp, log_n)
    dp_qb = Reduce(sems, g_qkv, r_qb, half, 3 * hd, 3, (1, 0, 2), dp, log_n, half)
    small_base = sems.take(2 + log_n)

    n_local = [0]
    pending = []

    def fetch(src, dst):
        cp = pltpu.make_async_copy(src, dst, local.at[n_local[0]])
        n_local[0] += 1
        cp.start()
        return cp

    x_loads = [
        [fetch(x_in.at[slot_rows(s, o)], x_mg.at[own_rows(s, o)]) for o in range(4)] for s in range(parts)
    ]
    w_out_load = fetch(w_out_in, w_out.at[pl.ds(pl.multiple_of(t * hd, hd), hd)])
    fc1_load = fetch(w_fc1_in, w_fc1)
    fc2_load = fetch(w_fc2_in, w_fc2)
    tg_loads = [
        fetch(og_in.at[slot_rows(s, o)], tg.at[own_rows(s, o)]) for s in range(parts) for o in range(4)
    ]

    barrier = pltpu.get_barrier_semaphore()
    for target in (sib, opp):
        pl.semaphore_signal(
            barrier, inc=1, device_id={"tensor": target}, device_id_type=pl.DeviceIdType.MESH
        )
    for b in range(log_n):
        step = 1 << b
        other = dp + step * (1 - 2 * lax.rem(dp // step, 2))
        pl.semaphore_signal(
            barrier, inc=1, device_id={"dp": other}, device_id_type=pl.DeviceIdType.MESH
        )
    pl.semaphore_wait(barrier, 2 + log_n)

    w_out_load.wait()
    ag_w.start(0)

    def row(ref):
        return ref[...].astype(f32).reshape(1, ref.shape[0])

    ln1_gain, ln1_shift, ln2_gain, ln2_shift, b_out, b_fc2, b_fc1 = [row(v) for v in vecs]
    b_q, b_v = b_qv[0:1, :].astype(f32), b_qv[1:2, :].astype(f32)

    ends, total = [], 0
    for i in range(lens.shape[0]):
        total = total + lens[i]
        ends.append(total)

    def segment_of(place):
        passed = jnp.zeros_like(place)
        for e in ends:
            passed = passed + jnp.where(place >= e, 1, 0)
        return jnp.where(place < ends[-1], passed, len(ends) + place)

    def positions(rows_of, c):
        n = c.shape[1]
        values = lax.broadcasted_iota(jnp.int32, (COORDS, n), 0)
        cols = []
        for i in range(3):
            hot = jnp.where(values == c[i : i + 1, :], 1.0, 0.0).astype(bf16)
            cols.append(mm_tn(jnp.concatenate([hot, hot, hot], axis=0), tab3[...]))
        return jnp.concatenate(cols, axis=1)

    def lane_blocks(ref, s):
        return jnp.concatenate([ref[:, slot_rows(s, o)] for o in range(4)], axis=1)

    def hidden_of(s):
        return x_mg[part_rows(s), :].astype(f32) + positions(None, lane_blocks(coords, s))

    for s in range(parts):
        for cp in x_loads[s]:
            cp.wait()

    def project(s, carry):
        for o in range(4):
            place = lax.broadcasted_iota(jnp.int32, (BLK, BLK), 0) + (o * parts * BLK + s * BLK)
            segk[own_rows(s, o), :] = segment_of(place)
        x_hat, _ = norm_parts(hidden_of(s))
        low = (x_hat * ln1_gain + ln1_shift).astype(bf16)
        n1[part_rows(s), :] = low
        proj = mm_nt(low, w_qkv[...])
        q = (proj[:, :hd] + b_q).astype(bf16).astype(f32).T.astype(bf16)
        k = proj[:, hd : 2 * hd].astype(bf16).astype(f32).T.astype(bf16)
        v = (proj[:, 2 * hd :] + b_v).astype(bf16).astype(f32).T.astype(bf16)
        for h in range(heads):
            head = slice(h * HEAD_DIM, (h + 1) * HEAD_DIM)
            q_t[h, :, part_rows(s)] = q[head]
            k_t[h, :, part_rows(s)] = k[head]
            v_t[h, :, part_rows(s)] = v[head]
            rows3[h, part_rows(s), :] = k[head].astype(f32).T.astype(bf16)
        return carry

    lax.fori_loop(0, parts, project, 0)

    def attend(s, carry):
        place = jnp.concatenate(
            [
                lax.broadcasted_iota(jnp.int32, (1, BLK), 1) + (o * parts * BLK + s * BLK)
                for o in range(4)
            ],
            axis=1,
        )
        allowed = segk[...][:, :1] == segment_of(place)
        for h in range(heads):
            scores = mm(rows3[h], q_t[h, :, part_rows(s)])
            scores = jnp.where(allowed, scores * (LOG2E / HEAD_DIM**0.5), MASK_FILL)
            top = jnp.max(scores, axis=0, keepdims=True)
            raised = jnp.exp2(scores - top)
            inv = 1.0 / jnp.sum(raised, axis=0, keepdims=True)
            low = raised.astype(bf16)
            probs[h, :, part_rows(s)] = low
            linv[h, :, part_rows(s)] = inv
            mixed = mm(v_t[h], low) * inv
            mix[s, pl.ds(pl.multiple_of(t * hd + h * HEAD_DIM, HEAD_DIM), HEAD_DIM), :] = mixed.astype(bf16)
        ag_mix.start(s)

        @pl.when(s >= 1)
        def _():
            ag_mix.forward(s - 1)

        return carry

    lax.fori_loop(0, parts, attend, 0)
    ag_w.forward(0)
    for cp in tg_loads:
        cp.wait()
    fc1_load.wait()
    fc2_load.wait()
    ag_w.finish(0)
    fc1_sums[...] = jnp.zeros_like(fc1_sums)
    small[0] = jnp.zeros_like(small[0])

    def visible_rows(s, owner):
        return segk[own_rows(s, owner), :][:, :1] < len(ends)

    def second_norm_back(s):
        u = rs_n2.finish(s)
        middle = mid_own[s]
        x_hat, r = norm_parts(middle)
        grad = tg[own_rows(s, t), :].astype(f32) + norm_back(u, ln2_gain, x_hat, r)
        mg_own[s] = grad
        small[0, 2:3, :] += jnp.sum(u * x_hat, axis=0, keepdims=True)
        small[0, 3:4, :] += jnp.sum(u, axis=0, keepdims=True)
        small[0, 4:5, :] += jnp.sum(grad, axis=0, keepdims=True)
        small[0, 5:6, :] += jnp.sum(tg[own_rows(s, t), :].astype(f32), axis=0, keepdims=True)
        x_mg[own_rows(s, t), :] = grad.astype(bf16)
        ag_mg.start(s)

    def feed(s, carry):
        @pl.when(s == parts - 1)
        def _():
            ag_mix.forward(s)

        ag_mix.finish(s)
        attn = mm_tn(mix[s], w_out[...])
        middle = hidden_of(s) + attn + b_out
        mine = middle[:BLK]
        for o in range(1, 4):
            mine = jnp.where(t == o, middle[o * BLK : (o + 1) * BLK], mine)
        mid_own[s] = mine
        x_hat, _ = norm_parts(middle)
        low = (x_hat * ln2_gain + ln2_shift).astype(bf16)
        n2_oi[part_rows(s), :] = low
        value, slope = gelu_pair(mm(low, w_fc1[...]) + b_fc1)
        act_ol[part_rows(s), :] = value.astype(bf16)
        shown = segk[part_rows(s), :][:, :1] < len(ends)
        top = jnp.where(shown, tg[part_rows(s), :].astype(f32), 0.0).astype(bf16)
        tg[part_rows(s), :] = top
        pre = (mm_nt(top, w_fc2[...]) * slope).astype(bf16)
        pg_dq[part_rows(s), :] = pre
        fc1_sums[0:1, :] += jnp.sum(pre.astype(f32), axis=0, keepdims=True)
        rs_n2.store(s, mm_nt(pre, w_fc1[...]))
        rs_n2.start(s)

        @pl.when(s >= 1)
        def _():
            second_norm_back(s - 1)

        @pl.when(s >= 2)
        def _():
            ag_mg.forward(s - 2)

        rs_mlp.store(s, mm(act_ol[part_rows(s), :], w_fc2[...]))
        rs_n2.across(s)
        return carry

    lax.fori_loop(0, parts, feed, 0)

    def weight_grad(dst, left, right, cols, first=0, last=None):
        last = left.shape[1] if last is None else last
        for i in range(first, last, 256 if (last - first) % 256 == 0 else last - first):
            n = 256 if (last - first) % 256 == 0 else last - first
            dst[i : i + n, :cols] = mm_tn(left[:, i : i + n], right[:, :cols]).astype(bf16)

    s_fc2, s_fc1, s_wout = dp_fc2.steps(), dp_fc1.steps(), dp_wout.steps()
    s_qa, s_qb = dp_qa.steps(), dp_qb.steps()

    def go(*chains):
        for steps in chains:
            if steps:
                steps.pop(0)()

    weight_grad(g_fc2, act_ol, tg, width)
    go(s_fc2)
    for s in range(parts):
        rs_mlp.start(s)
    second_norm_back(parts - 1)
    x_own_loads = [fetch(x_in.at[slot_rows(s, t)], tg.at[own_rows(s, t)]) for s in range(parts)]
    if parts >= 2:
        ag_mg.forward(parts - 2)
    for s in range(parts):
        rs_mlp.across(s)
    weight_grad(g_fc1, n2_oi, pg_dq, width)
    go(s_fc1)
    ag_mg.forward(parts - 1)
    for s in range(parts):
        ag_mg.finish(s)

    def layer_out(s):
        total = mid_own[s] + rs_mlp.finish(s) + b_fc2
        act_ol[slot_rows(s, t), :] = jnp.where(visible_rows(s, t), total, 0.0).astype(bf16)
        ag_out.start(s)

    for s in range(parts):
        rows = part_rows(s)
        own = pl.ds(pl.multiple_of(t * hd, hd), hd)
        low = mm_nt(x_mg[rows, :], w_out[own, :]).astype(bf16).astype(f32).T
        for h in range(heads):
            scaled = (low[h * HEAD_DIM : (h + 1) * HEAD_DIM] * linv[h, :, rows]).astype(bf16)
            do_t[h, :, rows] = scaled
            mixed = mix[s, pl.ds(pl.multiple_of(t * hd + h * HEAD_DIM, HEAD_DIM), HEAD_DIM), :]
            delta[h, :, rows] = jnp.sum(scaled.astype(f32) * mixed.astype(f32), axis=0, keepdims=True)
    own = pl.ds(pl.multiple_of(t * hd, hd), hd)
    grad_out = mm(mix[0, own, :], x_mg[part_rows(0), :])
    for s in range(1, parts):
        grad_out = grad_out + mm(mix[s, own, :], x_mg[part_rows(s), :])
    g_wout[...] = grad_out.astype(bf16)
    go(s_wout)

    for h in range(heads):
        rows3[0] = v_t[h].astype(f32).T.astype(bf16)
        rows3[1] = q_t[h].astype(f32).T.astype(bf16)
        rows3[2] = do_t[h].astype(f32).T.astype(bf16)

        def back(s, carry, h=h):
            rows = part_rows(s)
            p = probs[h, rows, :]
            wg = mm(rows3[0, rows, :], do_t[h])
            sg = (p.astype(f32) * (wg - delta[h])).astype(bf16)
            dv = mm(p, rows3[2])
            dk = mm(sg, rows3[1]) * (1.0 / HEAD_DIM**0.5)
            pg_dq[rows, hd + h * HEAD_DIM : hd + (h + 1) * HEAD_DIM] = dk.astype(bf16)
            pg_dq[rows, 2 * hd + h * HEAD_DIM : 2 * hd + (h + 1) * HEAD_DIM] = dv.astype(bf16)
            dq = mm(k_t[h, :, rows], sg)

            @pl.when(s == 0)
            def _():
                acc[...] = dq

            @pl.when(s > 0)
            def _():
                acc[...] += dq

            return carry

        lax.fori_loop(0, parts, back, 0)
        pg_dq[:, h * HEAD_DIM : (h + 1) * HEAD_DIM] = (acc[...].T * (1.0 / HEAD_DIM**0.5)).astype(bf16)
        go(s_fc2, s_fc1)
        if h == 0:
            layer_out(0)
        if h == 1:
            go(s_wout)
            for s in range(1, parts):
                layer_out(s)
        if h == heads - 1:
            go(s_wout)
            for s in range(parts):
                ag_out.forward(s)

    for s in range(parts):
        rs_n1.store(s, mm(pg_dq[part_rows(s), : 3 * hd], w_qkv[...]))
        rs_n1.start(s)
        if s >= 1:
            rs_n1.across(s - 1)
        if s == 0:
            weight_grad(g_qkv, n1, pg_dq, 3 * hd, 0, half)
            go(s_qa)
        if s == 1:
            weight_grad(g_qkv, n1, pg_dq, 3 * hd, half, width)
            go(s_qb)
    rs_n1.across(parts - 1)
    go(s_fc2, s_fc1, s_wout)
    sums = jnp.sum(pg_dq[:, : 3 * hd].astype(f32), axis=0, keepdims=True)
    small[0, 8:9, :] = fc1_sums[0:1, :]
    small[0, 9:10, :hd] = sums[:, :hd]
    small[0, 10:11, :hd] = sums[:, 2 * hd :]

    def first_norm_back(s):
        u = rs_n1.finish(s)
        hidden = tg[own_rows(s, t), :].astype(f32) + positions(None, coords[:, slot_rows(s, t)])
        x_hat, r = norm_parts(hidden)
        grad = mg_own[s] + norm_back(u, ln1_gain, x_hat, r)
        small[0, 0:1, :] += jnp.sum(u * x_hat, axis=0, keepdims=True)
        small[0, 1:2, :] += jnp.sum(u, axis=0, keepdims=True)
        n2_oi[slot_rows(s, t), :] = grad.astype(bf16)
        ag_in.start(s)

    hops = [(8, {"tensor": sib}), (8, {"tensor": opp})]
    for b in range(log_n):
        step = 1 << b
        hops.append((16, {"dp": dp + step * (1 - 2 * lax.rem(dp // step, 2))}))

    def small_copy(i):
        rows, target = hops[i]
        return remote(
            sems, small_base + i, small.at[i, pl.ds(0, rows)], small_got.at[i, pl.ds(0, rows)], target
        )

    def small_add(i):
        rows = hops[i][0]
        small_copy(i).wait()
        small[i + 1, 0:rows] = small[i, 0:rows] + small_got[i, 0:rows]
        if rows < 16:
            small[i + 1, rows:16] = small[i, rows:16]
        if i + 1 < len(hops):
            small_copy(i + 1).start()

    for cp in x_own_loads:
        cp.wait()
    for s in range(parts):
        first_norm_back(s)
        if s >= 1:
            ag_in.forward(s - 1)
        if s == 0:
            go(s_fc2, s_fc1, s_wout)
        if s == 1:
            go(s_qa, s_qb)
    small_copy(0).start()
    go(s_fc2, s_fc1)
    small_add(0)
    go(s_qa, s_qb)
    small_add(1)
    ag_in.forward(parts - 1)
    i = 2
    while s_qa or s_qb or s_fc2 or s_fc1 or s_wout:
        go(s_qa, s_qb, s_wout, s_fc2, s_fc1)
        if i < len(hops):
            small_add(i)
            i += 1
    for j in range(i, len(hops)):
        small_add(j)

    outs = [
        fetch(g_fc2, out_fc2),
        fetch(g_fc1, out_fc1),
        fetch(g_wout, out_wout),
        fetch(g_qkv, out_qkv),
        fetch(small.at[len(hops)], out_small),
    ]
    for s in range(parts):
        ag_out.finish(s)
    outs.append(fetch(act_ol, out_layer))
    for s in range(parts):
        ag_in.finish(s)
    outs.append(fetch(n2_oi, out_input))
    for cp in outs:
        cp.wait()


def sincos_rows(feature_count):
    half_width = feature_count // 6
    ladder = np.arange(half_width, dtype=np.float32) / np.float32(half_width)
    frequency = np.power(np.float32(10000.0), -ladder).astype(np.float32)
    angles = (np.arange(COORDS, dtype=np.float32)[:, None] * frequency[None, :]).astype(np.float32)
    wide = angles.astype(np.float64)
    left = np.concatenate([np.sin(wide), np.cos(wide)], axis=1)
    terms = []
    for _ in range(3):
        terms.append(left.astype(np.float32).astype(ml_dtypes.bfloat16))
        left = left - terms[-1].astype(np.float64)
    return jnp.asarray(np.concatenate(terms, axis=0))


def on_device(
    n_dp,
    layer_input,
    patch_coords,
    item_lengths,
    out_grad,
    ln1_gain,
    ln1_shift,
    w_qkv,
    b_qv,
    w_out,
    b_out,
    ln2_gain,
    ln2_shift,
    w_fc1,
    b_fc1,
    w_fc2,
    b_fc2,
):
    tokens, width = layer_input.shape
    hd = w_out.shape[0]
    ff = w_fc1.shape[1]
    heads = hd // HEAD_DIM
    parts = tokens // (4 * BLK)
    log_n = n_dp.bit_length() - 1
    size = 4 * BLK
    got = Reduce.got_rows
    vmem = lambda *s: pltpu.VMEM(s, bf16)
    vmem32 = lambda *s: pltpu.VMEM(s, f32)
    scratch = [
        vmem(tokens, width),
        vmem(tokens, width),
        vmem(tokens, width),
        vmem(heads, HEAD_DIM, tokens),
        vmem(heads, HEAD_DIM, tokens),
        vmem(heads, HEAD_DIM, tokens),
        vmem(heads, tokens, HEAD_DIM),
        vmem(heads, tokens, tokens),
        vmem(parts, 4 * hd, size),
        vmem32(heads, 1, tokens),
        vmem(4 * hd, width),
        vmem(width, ff),
        vmem(ff, width),
        vmem32(parts, BLK, width),
        vmem(tokens, width),
        vmem(tokens, width),
        vmem(tokens, width),
    ]
    for _ in range(2):
        scratch += [
            vmem(parts, 2, 2, BLK, width),
            vmem(parts, 2, BLK, width),
            vmem(parts, BLK, width),
        ]
    scratch += [
        vmem32(parts, BLK, width),
        vmem(heads, HEAD_DIM, tokens),
        vmem32(heads, 1, tokens),
        vmem32(HEAD_DIM, tokens),
        vmem(ff, width),
        vmem(width, ff),
        vmem(hd, width),
        vmem(width, 3 * hd),
        vmem(got(ff, 3, log_n), width),
        vmem(got(width, 3, log_n), width),
        vmem(got(hd, 2, log_n), width),
        vmem(got(width // 2, 3, log_n), 3 * hd),
        vmem(got(width // 2, 3, log_n), 3 * hd),
        pltpu.VMEM((tokens, BLK), jnp.int32),
        vmem32(3 + log_n, 16, width),
        vmem32(2 + log_n, 16, width),
        vmem32(8, ff),
    ]
    n_sems = 3 + 4 * 3 * parts + 3 * 2 * parts + 4 * (log_n + 3) + (log_n + 2) + 2 + log_n
    scratch += [
        pltpu.SemaphoreType.DMA((n_sems,)),
        pltpu.SemaphoreType.DMA((n_sems,)),
        pltpu.SemaphoreType.REGULAR((14,)),
        pltpu.SemaphoreType.DMA((4 * parts * 2 + parts + 3 + 7,)),
    ]
    shape = jax.ShapeDtypeStruct
    hbm = pl.BlockSpec(memory_space=pl.ANY)
    here = pl.BlockSpec(memory_space=pltpu.VMEM)
    results = pl.pallas_call(
        functools.partial(layer_kernel, (parts, log_n, heads)),
        name="layer",
        out_shape=(
            shape((tokens, width), bf16),
            shape((tokens, width), bf16),
            shape((ff, width), bf16),
            shape((width, ff), bf16),
            shape((hd, width), bf16),
            shape((width, 3 * hd), bf16),
            shape((16, width), f32),
        ),
        in_specs=[pl.BlockSpec(memory_space=pltpu.SMEM), hbm, hbm, here, here, hbm, hbm, hbm] + [here] * 9,
        out_specs=(hbm,) * 7,
        scratch_shapes=scratch,
        compiler_params=pltpu.CompilerParams(
            collective_id=0, has_side_effects=True, vmem_limit_bytes=67043328
        ),
    )(
        item_lengths,
        layer_input,
        out_grad,
        patch_coords,
        w_qkv.reshape(width, 3 * hd).T,
        w_out,
        w_fc1,
        w_fc2,
        ln1_gain,
        ln1_shift,
        ln2_gain,
        ln2_shift,
        b_out,
        b_fc2,
        b_fc1,
        b_qv,
        sincos_rows(width),
    )
    layer_output, input_grad, g_fc2, g_fc1, g_wout, g_qkv, small = results
    return (
        layer_output,
        input_grad.astype(f32),
        small[0],
        small[1],
        g_qkv.astype(f32).reshape(width, 3, hd),
        small[9:11, :hd],
        g_wout.astype(f32),
        small[4],
        small[2],
        small[3],
        g_fc1.astype(f32),
        small[8, :ff],
        g_fc2.astype(f32),
        small[5],
    )


def solution(mesh):
    placed = (
        P("dp", None),
        P(None, "dp"),
        P("dp"),
        P("dp", None),
        P(),
        P(),
        P(None, None, "tensor"),
        P(None, "tensor"),
        P("tensor", None),
        P(),
        P(),
        P(),
        P(None, "tensor"),
        P("tensor"),
        P("tensor", None),
        P(),
    )
    return jax.shard_map(
        functools.partial(on_device, mesh.shape["dp"]),
        mesh=mesh,
        in_specs=placed,
        out_specs=(
            P("dp", None),
            P("dp", None),
            P(),
            P(),
            P(None, None, "tensor"),
            P(None, "tensor"),
            P("tensor", None),
            P(),
            P(),
            P(),
            P(None, "tensor"),
            P("tensor"),
            P("tensor", None),
            P(),
        ),
        check_vma=False,
    )
```

```python
import functools

import jax
import jax.numpy as jnp
import ml_dtypes
import numpy as np
from jax import lax
from jax.experimental import pallas as pl
from jax.experimental.pallas import tpu as pltpu
from jax.sharding import PartitionSpec as P

HEAD_DIM = 64
NORM_EPS = 1e-06
MASK_FILL = -1e30
LOG2E = 1.4426950408889634
BLK = 128
COORDS = 64
BEFORE_ATTENTION = ["wg2", "f2a", "f2b", "f2c", "n2b", "mla", "f2a", "f2b", "wg1a", "wg1b", "f2c", "wg1c", "f1a", "f1b", "f1c", "f2a", "f2b", "mgf", "md0", "md1", "f2c", "md2", "f2a", "gw", "w"]
IN_ATTENTION = (
    [["lo0", "f2b", "f1a"], ["lo1", "f2a", "f2c", "f1b", "w"], ["f2b"]],
    [["lo2", "f2c", "f1a", "f2a", "f1c", "f1b"], ["of0", "f2b", "w"], ["f2c"]],
    [["of1", "f1a"], ["f2b"], ["of2", "f2a"]],
)
AFTER_ATTENTION = ["st0", "f1c", "wqa", "qa", "f2c", "f1b", "st1", "w", "na0", "wqb", "qb", "wqc", "qc", "f1a", "st2", "na1", "f1c", "sums", "qa", "f1b", "na2", "w", "f1a", "nb0", "f1c", "qa", "qb", "f1b", "nb1", "fo", "qc", "w", "nb2", "sm", "f1c", "f1a", "qa", "sm", "qb", "if0", "qc", "f1b", "qa", "qb", "qc", "if1", "fi0", "qa", "f1c", "qb", "qc", "if2", "fi1", "sm", "qb", "qa", "qc", "sm", "sm", "qb", "qc", "sm"]
f32 = jnp.float32
bf16 = jnp.bfloat16


def mm(a, b):
    return lax.dot_general(a, b, (((1,), (0,)), ((), ())), preferred_element_type=f32)


def mm_nt(a, b):
    return lax.dot_general(a, b, (((1,), (1,)), ((), ())), preferred_element_type=f32)


def mm_tn(a, b):
    return lax.dot_general(a, b, (((0,), (0,)), ((), ())), preferred_element_type=f32)


def norm_parts(v):
    width = v.shape[-1]
    mean = jnp.sum(v, axis=-1, keepdims=True) * (1.0 / width)
    centred = v - mean
    spread = jnp.sum(centred * centred, axis=-1, keepdims=True) * (1.0 / width)
    r = lax.rsqrt(spread + NORM_EPS)
    return centred * r, r


def norm_back(u, gain, x_hat, r):
    width = u.shape[-1]
    ug = u * gain
    m1 = jnp.sum(ug, axis=-1, keepdims=True) * (1.0 / width)
    m2 = jnp.sum(ug * x_hat, axis=-1, keepdims=True) * (1.0 / width)
    return r * (ug - m1 - x_hat * m2)


def gelu_pair(v):
    phi = 0.5 * (1.0 + lax.erf(v * 0.7071067811865476))
    dens = jnp.exp(-0.5 * v * v) * 0.3989422804014327
    return v * phi, phi + v * dens


class Sems:
    def __init__(self):
        self.count = 0
        self.ready_count = 0
        self.ready = None
        self.one = None
        self.send = None
        self.recv = None

    def take(self, n=1):
        first = self.count
        self.count += n
        return first


def remote(sems, idx, src, dst, target):
    return pltpu.make_async_remote_copy(
        src_ref=src,
        dst_ref=dst,
        send_sem=sems.send.at[idx],
        recv_sem=sems.recv.at[idx],
        device_id=target,
        device_id_type=pl.DeviceIdType.MESH,
    )


class Gather:
    def __init__(self, sems, parts, view, t):
        self.sems, self.view, self.t = sems, view, t
        self.base = sems.take(3 * parts)
        self.parts = parts
        self.sib = t + 1 - 2 * lax.rem(t, 2)
        self.opp = lax.rem(t + 2, 4)

    def copy(self, kind, s, owner):
        ref = self.view(s, owner)
        target = {"tensor": self.opp if kind == 1 else self.sib}
        return remote(self.sems, self.base + kind * self.parts + s, ref, ref, target)

    def start(self, s):
        self.copy(1, s, self.t).start()
        self.copy(0, s, self.t).start()

    def forward(self, s):
        self.copy(1, s, self.opp).wait_recv()
        self.copy(2, s, self.opp).start()

    def finish(self, s):
        self.copy(0, s, self.sib).wait_recv()
        self.copy(2, s, lax.rem(self.sib + 2, 4)).wait_recv()
        self.copy(0, s, self.t).wait_send()
        self.copy(1, s, self.t).wait_send()
        self.copy(2, s, self.opp).wait_send()


class Scatter:
    def __init__(self, sems, parts, bufs, t):
        self.part, self.got_a, self.got_b = bufs
        self.sems = sems
        self.base = sems.take(2 * parts)
        self.parts = parts
        self.core = lax.rem(t, 2)
        self.chip = t // 2
        self.sib = t + 1 - 2 * lax.rem(t, 2)
        self.opp = lax.rem(t + 2, 4)

    def store(self, s, value):
        for o in range(4):
            self.part[s, o % 2, o // 2] = value[o * BLK : (o + 1) * BLK].astype(bf16)

    def copy_a(self, s):
        return remote(
            self.sems, self.base + s, self.part.at[s, 1 - self.core], self.got_a.at[s], {"tensor": self.sib}
        )

    def copy_b(self, s):
        return remote(
            self.sems,
            self.base + self.parts + s,
            self.part.at[s, self.core, 1 - self.chip],
            self.got_b.at[s],
            {"tensor": self.opp},
        )

    def start(self, s):
        self.copy_a(s).start()

    def across(self, s):
        self.copy_a(s).wait()
        other = 1 - self.chip
        self.part[s, self.core, other] = (
            self.part[s, self.core, other].astype(f32) + self.got_a[s, other].astype(f32)
        ).astype(bf16)
        self.copy_b(s).start()

    def finish(self, s):
        self.copy_b(s).wait()
        return (
            self.part[s, self.core, self.chip].astype(f32)
            + self.got_a[s, self.chip].astype(f32)
            + self.got_b[s].astype(f32)
        )


class Reduce:
    def __init__(self, sems, ref, got, rows, cols, halvings, order, dp, log_n, first=0, spot=0):
        self.sems, self.ref, self.got, self.cols = sems, ref, got, cols
        rest = [b for b in range(log_n) if b not in order[:halvings]]
        self.bits = list(order[:halvings]) + rest
        self.halvings = halvings
        self.partners = [dp + (1 << b) * (1 - 2 * lax.rem(dp // (1 << b), 2)) for b in self.bits]
        self.base = sems.take(len(self.bits) + halvings)
        self.ready = sems.ready_count
        sems.ready_count += halvings
        self.low, self.size, self.spot = [first], [rows], []
        at = spot
        for j, b in enumerate(self.bits):
            side = lax.rem(dp // (1 << b), 2)
            if j < halvings:
                half = self.size[-1] // 2
                self.low.append(self.low[-1] + side * half)
                self.size.append(half)
            else:
                self.low.append(self.low[-1])
                self.size.append(self.size[-1])
            self.spot.append(at)
            at += self.size[-1]

    @staticmethod
    def got_rows(rows, halvings, log_n):
        return sum(rows >> (j + 1) for j in range(halvings)) + (log_n - halvings) * (rows >> halvings)

    def partner(self, j):
        return {"dp": self.partners[j]}

    def at(self, ref, low, size):
        if not isinstance(low, int):
            low = pl.multiple_of(low, 16)
        return ref.at[pl.ds(low, size), pl.ds(0, self.cols)]

    def copy_in(self, j):
        size = self.size[j + 1]
        if j < self.halvings:
            other = self.low[j] + self.low[j] + size - self.low[j + 1]
        else:
            other = self.low[j]
        return remote(
            self.sems,
            self.base + j,
            self.at(self.ref, other, size),
            self.at(self.got, self.spot[j], size),
            self.partner(j),
        )

    def copy_back(self, j):
        here = self.at(self.ref, self.low[j + 1], self.size[j + 1])
        return remote(self.sems, self.base + len(self.bits) + j, here, here, self.partner(j))

    def copy_home(self, j):
        size = self.size[j + 1]
        other = self.low[j] + self.low[j] + size - self.low[j + 1]
        here = self.at(self.ref, other, size)
        return remote(self.sems, self.base + len(self.bits) + j, here, here, self.partner(j))

    def begin(self, j):
        self.copy_in(j).start()

    def add(self, j):
        self.copy_in(j).wait()
        if j < self.halvings:
            pl.semaphore_signal(
                self.sems.ready.at[self.ready + j],
                inc=self.sems.one,
                device_id=self.partner(j),
                device_id_type=pl.DeviceIdType.MESH,
            )
        mine = self.at(self.ref, self.low[j + 1], self.size[j + 1])
        theirs = self.at(self.got, self.spot[j], self.size[j + 1])
        mine[...] = (mine[...].astype(f32) + theirs[...].astype(f32)).astype(bf16)

    def give(self, j):
        pl.semaphore_wait(self.sems.ready.at[self.ready + j], self.sems.one)
        self.copy_back(j).start()

    def take(self, j):
        self.copy_back(j).wait_send()
        self.copy_home(j).wait_recv()

    def steps(self):
        out = [lambda: self.begin(0)]
        n = len(self.bits)
        for j in range(n):

            def step(j=j):
                self.add(j)
                if j + 1 < n:
                    self.begin(j + 1)
                else:
                    self.give(self.halvings - 1)

            out.append(step)
        for j in reversed(range(self.halvings)):

            def back(j=j):
                self.take(j)
                if j > 0:
                    self.give(j - 1)

            out.append(back)
        return out


def layer_kernel(
    geo,
    lens,
    x_in,
    og_in,
    coords,
    w_qkv,
    w_out_in,
    w_fc1_in,
    w_fc2_in,
    v0,
    v1,
    v2,
    v3,
    v4,
    v5,
    v6,
    b_qv,
    tab3,
    out_layer,
    out_input,
    out_fc2,
    out_fc1,
    out_wout,
    out_qkv,
    out_small,
    x_mg,
    tg,
    n1,
    q_t,
    k_t,
    v_t,
    rows3,
    probs,
    mix,
    linv,
    w_out,
    w_fc1,
    w_fc2,
    mid_own,
    n2_oi,
    act_ol,
    pg_dq,
    part0,
    got_a0,
    got_b0,
    part1,
    got_a1,
    got_b1,
    mg_own,
    do_t,
    delta,
    acc,
    g_fc2,
    g_fc1,
    g_wout,
    g_qkv,
    r_fc2,
    r_fc1,
    r_wout,
    r_qkv,
    segk,
    small,
    small_got,
    fc1_sums,
    send,
    recv,
    ready,
    local,
):
    parts, log_n, heads = geo
    vecs = (v0, v1, v2, v3, v4, v5, v6)
    size = 4 * BLK
    dp = lax.axis_index("dp")
    t = lax.axis_index("tensor")
    sib = t + 1 - 2 * lax.rem(t, 2)
    opp = lax.rem(t + 2, 4)
    width = x_mg.shape[1]
    hd = heads * HEAD_DIM

    sems = Sems()
    sems.send, sems.recv, sems.ready = send, recv, ready
    sems.one = lax.rem(t, 1) + 1

    def part_rows(s):
        return pl.ds(pl.multiple_of(s * size, size), size)

    def own_rows(s, owner):
        return pl.ds(pl.multiple_of(s * size + owner * BLK, BLK), BLK)

    def slot_rows(s, owner):
        return pl.ds(pl.multiple_of(owner * (parts * BLK) + s * BLK, BLK), BLK)

    ag_w = Gather(sems, 1, lambda s, o: w_out.at[pl.ds(pl.multiple_of(o * hd, hd), hd)], t)
    ag_mix = Gather(sems, parts, lambda s, o: mix.at[s, pl.ds(pl.multiple_of(o * hd, hd), hd)], t)
    ag_mg = Gather(sems, parts, lambda s, o: x_mg.at[own_rows(s, o)], t)
    ag_out = Gather(sems, parts, lambda s, o: act_ol.at[slot_rows(s, o)], t)
    ag_in = Gather(sems, parts, lambda s, o: n2_oi.at[slot_rows(s, o)], t)
    rs_n2 = Scatter(sems, parts, (part0, got_a0, got_b0), t)
    rs_mlp = Scatter(sems, parts, (part1, got_a1, got_b1), t)
    rs_n1 = Scatter(sems, parts, (part0, got_a0, got_b0), t)
    third = width // 3
    along_x, along_z = (0, 1, 2), (1, 0, 2)
    chains = {}

    def unit(name, ref, got, out, rows, cols, halvings, order, i=0):
        first, spot = i * rows, i * Reduce.got_rows(rows, halvings, log_n)
        total = Reduce(sems, ref, got, rows, cols, halvings, order, dp, log_n, first, spot)
        chains[name] = (total.steps(), ref, out, pl.ds(first, rows))

    for i in range(3):
        unit("f2" + "abc"[i], g_fc2, r_fc2, out_fc2, third, width, 3, along_x if i else along_z, i)
    for i in range(3):
        unit("f1" + "abc"[i], g_fc1, r_fc1, out_fc1, third, width, 3, along_x, i)
    unit("w", g_wout, r_wout, out_wout, hd, width, 2, along_z[:2])
    for i in range(3):
        unit("q" + "abc"[i], g_qkv, r_qkv, out_qkv, third, 3 * hd, 3, along_x, i)
    small_base = sems.take(2 + log_n)

    n_local = [0]
    pending = []

    def fetch(src, dst):
        cp = pltpu.make_async_copy(src, dst, local.at[n_local[0]])
        n_local[0] += 1
        cp.start()
        return cp

    x_loads = [
        [fetch(x_in.at[slot_rows(s, o)], x_mg.at[own_rows(s, o)]) for o in range(4)] for s in range(parts)
    ]
    w_out_load = fetch(w_out_in, w_out.at[pl.ds(pl.multiple_of(t * hd, hd), hd)])
    fc1_load = fetch(w_fc1_in, w_fc1)
    fc2_load = fetch(w_fc2_in, w_fc2)
    tg_loads = [
        fetch(og_in.at[slot_rows(s, o)], tg.at[own_rows(s, o)]) for s in range(parts) for o in range(4)
    ]

    barrier = pltpu.get_barrier_semaphore()
    for target in (sib, opp):
        pl.semaphore_signal(
            barrier, inc=1, device_id={"tensor": target}, device_id_type=pl.DeviceIdType.MESH
        )
    for b in range(log_n):
        step = 1 << b
        other = dp + step * (1 - 2 * lax.rem(dp // step, 2))
        pl.semaphore_signal(
            barrier, inc=1, device_id={"dp": other}, device_id_type=pl.DeviceIdType.MESH
        )
    pl.semaphore_wait(barrier, 2 + log_n)

    w_out_load.wait()
    ag_w.start(0)

    def row(ref):
        return ref[...].astype(f32).reshape(1, ref.shape[0])

    ln1_gain, ln1_shift, ln2_gain, ln2_shift, b_out, b_fc2, b_fc1 = [row(v) for v in vecs]
    b_q, b_v = b_qv[0:1, :].astype(f32), b_qv[1:2, :].astype(f32)

    ends, total = [], 0
    for i in range(lens.shape[0]):
        total = total + lens[i]
        ends.append(total)

    def segment_of(place):
        passed = jnp.zeros_like(place)
        for e in ends:
            passed = passed + jnp.where(place >= e, 1, 0)
        return jnp.where(place < ends[-1], passed, len(ends) + place)

    def positions(rows_of, c):
        n = c.shape[1]
        values = lax.broadcasted_iota(jnp.int32, (COORDS, n), 0)
        cols = []
        for i in range(3):
            hot = jnp.where(values == c[i : i + 1, :], 1.0, 0.0).astype(bf16)
            cols.append(mm_tn(jnp.concatenate([hot, hot, hot], axis=0), tab3[...]))
        return jnp.concatenate(cols, axis=1)

    def lane_blocks(ref, s):
        return jnp.concatenate([ref[:, slot_rows(s, o)] for o in range(4)], axis=1)

    def hidden_of(s):
        return x_mg[part_rows(s), :].astype(f32) + positions(None, lane_blocks(coords, s))

    for s in range(parts):
        for cp in x_loads[s]:
            cp.wait()

    def project(s, carry):
        for o in range(4):
            place = lax.broadcasted_iota(jnp.int32, (BLK, BLK), 0) + (o * parts * BLK + s * BLK)
            segk[own_rows(s, o), :] = segment_of(place)
        x_hat, _ = norm_parts(hidden_of(s))
        low = (x_hat * ln1_gain + ln1_shift).astype(bf16)
        n1[part_rows(s), :] = low
        proj = mm_nt(low, w_qkv[...])
        q = (proj[:, :hd] + b_q).astype(bf16).astype(f32).T.astype(bf16)
        k = proj[:, hd : 2 * hd].astype(bf16).astype(f32).T.astype(bf16)
        v = (proj[:, 2 * hd :] + b_v).astype(bf16).astype(f32).T.astype(bf16)
        for h in range(heads):
            head = slice(h * HEAD_DIM, (h + 1) * HEAD_DIM)
            q_t[h, :, part_rows(s)] = q[head]
            k_t[h, :, part_rows(s)] = k[head]
            v_t[h, :, part_rows(s)] = v[head]
            rows3[h, part_rows(s), :] = k[head].astype(f32).T.astype(bf16)
        return carry

    lax.fori_loop(0, parts, project, 0)
    ag_w.forward(0)

    def attend(s, carry):
        place = jnp.concatenate(
            [
                lax.broadcasted_iota(jnp.int32, (1, BLK), 1) + (o * parts * BLK + s * BLK)
                for o in range(4)
            ],
            axis=1,
        )
        allowed = segk[...][:, :1] == segment_of(place)
        for h in range(heads):
            scores = mm(rows3[h], q_t[h, :, part_rows(s)])
            scores = jnp.where(allowed, scores * (LOG2E / HEAD_DIM**0.5), MASK_FILL)
            top = jnp.max(scores, axis=0, keepdims=True)
            raised = jnp.exp2(scores - top)
            inv = 1.0 / jnp.sum(raised, axis=0, keepdims=True)
            low = raised.astype(bf16)
            probs[h, :, part_rows(s)] = low
            linv[h, :, part_rows(s)] = inv
            mixed = mm(v_t[h], low) * inv
            mix[s, pl.ds(pl.multiple_of(t * hd + h * HEAD_DIM, HEAD_DIM), HEAD_DIM), :] = mixed.astype(bf16)
        ag_mix.start(s)

        @pl.when(s >= 1)
        def _():
            ag_mix.forward(s - 1)

        return carry

    lax.fori_loop(0, parts, attend, 0)
    for cp in tg_loads:
        cp.wait()
    fc1_load.wait()
    fc2_load.wait()
    ag_w.finish(0)
    fc1_sums[...] = jnp.zeros_like(fc1_sums)
    small[0] = jnp.zeros_like(small[0])

    def visible_rows(s, owner):
        return segk[own_rows(s, owner), :][:, :1] < len(ends)

    def second_norm_back(s):
        u = rs_n2.finish(s)
        middle = mid_own[s]
        x_hat, r = norm_parts(middle)
        grad = tg[own_rows(s, t), :].astype(f32) + norm_back(u, ln2_gain, x_hat, r)
        mg_own[s] = grad
        small[0, 2:3, :] += jnp.sum(u * x_hat, axis=0, keepdims=True)
        small[0, 3:4, :] += jnp.sum(u, axis=0, keepdims=True)
        small[0, 4:5, :] += jnp.sum(grad, axis=0, keepdims=True)
        small[0, 5:6, :] += jnp.sum(tg[own_rows(s, t), :].astype(f32), axis=0, keepdims=True)
        x_mg[own_rows(s, t), :] = grad.astype(bf16)
        ag_mg.start(s)

    def feed(s, carry):
        ag_mix.finish(s)
        attn = mm_tn(mix[s], w_out[...])
        middle = hidden_of(s) + attn + b_out
        mine = middle[:BLK]
        for o in range(1, 4):
            mine = jnp.where(t == o, middle[o * BLK : (o + 1) * BLK], mine)
        mid_own[s] = mine
        x_hat, _ = norm_parts(middle)
        low = (x_hat * ln2_gain + ln2_shift).astype(bf16)
        n2_oi[part_rows(s), :] = low
        value, slope = gelu_pair(mm(low, w_fc1[...]) + b_fc1)
        act_ol[part_rows(s), :] = value.astype(bf16)
        shown = segk[part_rows(s), :][:, :1] < len(ends)
        top = jnp.where(shown, tg[part_rows(s), :].astype(f32), 0.0).astype(bf16)
        tg[part_rows(s), :] = top
        pre = (mm_nt(top, w_fc2[...]) * slope).astype(bf16)
        pg_dq[part_rows(s), :] = pre
        fc1_sums[0:1, :] += jnp.sum(pre.astype(f32), axis=0, keepdims=True)
        rs_n2.store(s, mm_nt(pre, w_fc1[...]))
        rs_n2.start(s)

        @pl.when(s >= 1)
        def _():
            second_norm_back(s - 1)

        @pl.when(s >= 2)
        def _():
            ag_mg.forward(s - 2)

        @pl.when(s == parts - 2)
        def _():
            ag_mix.forward(parts - 1)

        rs_mlp.store(s, mm(act_ol[part_rows(s), :], w_fc2[...]))
        rs_n2.across(s)
        return carry

    lax.fori_loop(0, parts, feed, 0)

    def weight_grad(dst, left, right, cols, first, last):
        for i in range(first, last):
            rows = slice(i * third, (i + 1) * third)
            dst[rows, :cols] = mm_tn(left[:, rows], right[:, :cols]).astype(bf16)

    own = pl.ds(pl.multiple_of(t * hd, hd), hd)
    outs, ended, x_own_loads = [], [], []

    def layer_out(s):
        total = mid_own[s] + rs_mlp.finish(s) + b_fc2
        act_ol[slot_rows(s, t), :] = jnp.where(visible_rows(s, t), total, 0.0).astype(bf16)
        ag_out.start(s)

    def mixed_grad(s):
        ag_mg.finish(s)
        rows = part_rows(s)
        low = mm_nt(x_mg[rows, :], w_out[own, :]).astype(bf16).astype(f32).T
        for h in range(heads):
            scaled = (low[h * HEAD_DIM : (h + 1) * HEAD_DIM] * linv[h, :, rows]).astype(bf16)
            do_t[h, :, rows] = scaled
            mixed = mix[s, pl.ds(pl.multiple_of(t * hd + h * HEAD_DIM, HEAD_DIM), HEAD_DIM), :]
            delta[h, :, rows] = jnp.sum(scaled.astype(f32) * mixed.astype(f32), axis=0, keepdims=True)

    def out_weight_grad():
        total = mm(mix[0, own, :], x_mg[part_rows(0), :])
        for s in range(1, parts):
            total = total + mm(mix[s, own, :], x_mg[part_rows(s), :])
        g_wout[...] = total.astype(bf16)

    def first_norm_back(s):
        if s == 0:
            for cp in x_own_loads:
                cp.wait()
        u = rs_n1.finish(s)
        hidden = tg[own_rows(s, t), :].astype(f32) + positions(None, coords[:, slot_rows(s, t)])
        x_hat, r = norm_parts(hidden)
        grad = mg_own[s] + norm_back(u, ln1_gain, x_hat, r)
        small[0, 0:1, :] += jnp.sum(u * x_hat, axis=0, keepdims=True)
        small[0, 1:2, :] += jnp.sum(u, axis=0, keepdims=True)
        n2_oi[slot_rows(s, t), :] = grad.astype(bf16)
        ag_in.start(s)

    def sums():
        total = jnp.sum(pg_dq[:, : 3 * hd].astype(f32), axis=0, keepdims=True)
        small[0, 8:9, :] = fc1_sums[0:1, :]
        small[0, 9:10, :hd] = total[:, :hd]
        small[0, 10:11, :hd] = total[:, 2 * hd :]

    hops = [(8, {"tensor": sib}), (8, {"tensor": opp})]
    for b in range(log_n):
        step = 1 << b
        hops.append((16, {"dp": dp + step * (1 - 2 * lax.rem(dp // step, 2))}))

    def small_copy(i):
        rows, target = hops[i]
        return remote(
            sems, small_base + i, small.at[i, pl.ds(0, rows)], small_got.at[i, pl.ds(0, rows)], target
        )

    def small_add(i):
        rows = hops[i][0]
        small_copy(i).wait()
        small[i + 1, 0:rows] = small[i, 0:rows] + small_got[i, 0:rows]
        if rows < 16:
            small[i + 1, rows:16] = small[i, rows:16]
        if i + 1 < len(hops):
            small_copy(i + 1).start()

    small_steps = [lambda: small_copy(0).start()] + [
        functools.partial(small_add, i) for i in range(len(hops))
    ]

    def input_out(s):
        ag_in.finish(s)
        for o in range(4):
            outs.append(fetch(n2_oi.at[slot_rows(s, o)], out_input.at[slot_rows(s, o)]))

    def do(token):
        kind, at = token[:2], token[2:]
        if token in chains:
            steps, ref, out, rows = chains[token]
            steps.pop(0)()
            if not steps:
                ended.append((ref, out, rows))
        elif token == "wg2":
            weight_grad(g_fc2, act_ol, tg, width, 0, 3)
            for s in range(parts):
                rs_mlp.start(s)
        elif token == "n2b":
            second_norm_back(parts - 1)
            for s in range(parts):
                x_own_loads.append(fetch(x_in.at[slot_rows(s, t)], tg.at[own_rows(s, t)]))
            ag_mg.forward(parts - 2)
        elif token == "mla":
            for s in range(parts):
                rs_mlp.across(s)
        elif kind == "wg":
            i = "abc".index(token[3])
            weight_grad(g_fc1, n2_oi, pg_dq, width, i, i + 1)
        elif token == "mgf":
            ag_mg.forward(parts - 1)
        elif kind == "md":
            mixed_grad(int(at))
        elif token == "gw":
            out_weight_grad()
        elif kind == "lo":
            layer_out(int(at))
        elif kind == "of":
            ag_out.forward(int(at))
        elif kind == "st":
            s = int(at)
            rs_n1.store(s, mm(pg_dq[part_rows(s), : 3 * hd], w_qkv[...]))
            rs_n1.start(s)
        elif kind == "na":
            rs_n1.across(int(at))
        elif kind == "wq":
            i = "abc".index(at)
            weight_grad(g_qkv, n1, pg_dq, 3 * hd, i, i + 1)
        elif kind == "nb":
            first_norm_back(int(at))
        elif kind == "if":
            ag_in.forward(int(at))
        elif kind == "fi":
            input_out(int(at))
        elif token == "sums":
            sums()
        elif token == "sm":
            small_steps.pop(0)()
        elif token == "fo":
            for s in range(parts):
                ag_out.finish(s)
            outs.append(fetch(act_ol, out_layer))

    def run(tokens, in_loop=False):
        for token in tokens:
            do(token)
            while ended and not in_loop:
                ref, out, rows = ended.pop(0)
                outs.append(fetch(ref.at[rows], out.at[rows]))

    run(BEFORE_ATTENTION)

    for h in range(heads):
        rows3[0] = v_t[h].astype(f32).T.astype(bf16)
        rows3[1] = q_t[h].astype(f32).T.astype(bf16)
        rows3[2] = do_t[h].astype(f32).T.astype(bf16)

        def back(s, carry, h=h):
            rows = part_rows(s)
            p = probs[h, rows, :]
            wg = mm(rows3[0, rows, :], do_t[h])
            sg = (p.astype(f32) * (wg - delta[h])).astype(bf16)
            dv = mm(p, rows3[2])
            dk = mm(sg, rows3[1]) * (1.0 / HEAD_DIM**0.5)
            pg_dq[rows, hd + h * HEAD_DIM : hd + (h + 1) * HEAD_DIM] = dk.astype(bf16)
            pg_dq[rows, 2 * hd + h * HEAD_DIM : 2 * hd + (h + 1) * HEAD_DIM] = dv.astype(bf16)
            dq = mm(k_t[h, :, rows], sg)

            @pl.when(s == 0)
            def _():
                acc[...] = dq

            @pl.when(s > 0)
            def _():
                acc[...] += dq

            for k in range(2):

                @pl.when(s == k)
                def _(k=k):
                    run(IN_ATTENTION[h][k], True)

            return carry

        lax.fori_loop(0, parts, back, 0)
        pg_dq[:, h * HEAD_DIM : (h + 1) * HEAD_DIM] = (acc[...].T * (1.0 / HEAD_DIM**0.5)).astype(bf16)
        run(IN_ATTENTION[h][2])

    run(AFTER_ATTENTION)
    while small_steps or any(chain[0] for chain in chains.values()):
        for name in ("qa", "qb", "qc", "f2a", "f2b", "f2c", "f1a", "f1b", "f1c", "w"):
            if chains[name][0]:
                run([name])
        if small_steps:
            do("sm")
    outs.append(fetch(small.at[len(hops)], out_small))
    input_out(parts - 1)
    for cp in outs:
        cp.wait()


def sincos_rows(feature_count):
    half_width = feature_count // 6
    ladder = np.arange(half_width, dtype=np.float32) / np.float32(half_width)
    frequency = np.power(np.float32(10000.0), -ladder).astype(np.float32)
    angles = (np.arange(COORDS, dtype=np.float32)[:, None] * frequency[None, :]).astype(np.float32)
    wide = angles.astype(np.float64)
    left = np.concatenate([np.sin(wide), np.cos(wide)], axis=1)
    terms = []
    for _ in range(3):
        terms.append(left.astype(np.float32).astype(ml_dtypes.bfloat16))
        left = left - terms[-1].astype(np.float64)
    return jnp.asarray(np.concatenate(terms, axis=0))


def on_device(
    n_dp,
    layer_input,
    patch_coords,
    item_lengths,
    out_grad,
    ln1_gain,
    ln1_shift,
    w_qkv,
    b_qv,
    w_out,
    b_out,
    ln2_gain,
    ln2_shift,
    w_fc1,
    b_fc1,
    w_fc2,
    b_fc2,
):
    tokens, width = layer_input.shape
    hd = w_out.shape[0]
    ff = w_fc1.shape[1]
    heads = hd // HEAD_DIM
    parts = tokens // (4 * BLK)
    log_n = n_dp.bit_length() - 1
    size = 4 * BLK
    got = Reduce.got_rows
    vmem = lambda *s: pltpu.VMEM(s, bf16)
    vmem32 = lambda *s: pltpu.VMEM(s, f32)
    scratch = [
        vmem(tokens, width),
        vmem(tokens, width),
        vmem(tokens, width),
        vmem(heads, HEAD_DIM, tokens),
        vmem(heads, HEAD_DIM, tokens),
        vmem(heads, HEAD_DIM, tokens),
        vmem(heads, tokens, HEAD_DIM),
        vmem(heads, tokens, tokens),
        vmem(parts, 4 * hd, size),
        vmem32(heads, 1, tokens),
        vmem(4 * hd, width),
        vmem(width, ff),
        vmem(ff, width),
        vmem32(parts, BLK, width),
        vmem(tokens, width),
        vmem(tokens, width),
        vmem(tokens, width),
    ]
    for _ in range(2):
        scratch += [
            vmem(parts, 2, 2, BLK, width),
            vmem(parts, 2, BLK, width),
            vmem(parts, BLK, width),
        ]
    scratch += [
        vmem32(parts, BLK, width),
        vmem(heads, HEAD_DIM, tokens),
        vmem32(heads, 1, tokens),
        vmem32(HEAD_DIM, tokens),
        vmem(ff, width),
        vmem(width, ff),
        vmem(hd, width),
        vmem(width, 3 * hd),
        vmem(3 * got(width // 3, 3, log_n), width),
        vmem(3 * got(width // 3, 3, log_n), width),
        vmem(got(hd, 2, log_n), width),
        vmem(3 * got(width // 3, 3, log_n), 3 * hd),
        pltpu.VMEM((tokens, BLK), jnp.int32),
        vmem32(3 + log_n, 16, width),
        vmem32(2 + log_n, 16, width),
        vmem32(8, ff),
    ]
    n_sems = 3 + 4 * 3 * parts + 3 * 2 * parts + 9 * (log_n + 3) + (log_n + 2) + 2 + log_n
    scratch += [
        pltpu.SemaphoreType.DMA((n_sems,)),
        pltpu.SemaphoreType.DMA((n_sems,)),
        pltpu.SemaphoreType.REGULAR((29,)),
        pltpu.SemaphoreType.DMA((4 * parts * 2 + parts + 3 + 10 + 2 + 4 * parts,)),
    ]
    shape = jax.ShapeDtypeStruct
    hbm = pl.BlockSpec(memory_space=pl.ANY)
    here = pl.BlockSpec(memory_space=pltpu.VMEM)
    results = pl.pallas_call(
        functools.partial(layer_kernel, (parts, log_n, heads)),
        name="layer",
        out_shape=(
            shape((tokens, width), bf16),
            shape((tokens, width), bf16),
            shape((ff, width), bf16),
            shape((width, ff), bf16),
            shape((hd, width), bf16),
            shape((width, 3 * hd), bf16),
            shape((16, width), f32),
        ),
        in_specs=[pl.BlockSpec(memory_space=pltpu.SMEM), hbm, hbm, here, here, hbm, hbm, hbm] + [here] * 9,
        out_specs=(hbm,) * 7,
        scratch_shapes=scratch,
        compiler_params=pltpu.CompilerParams(
            collective_id=0, has_side_effects=True, vmem_limit_bytes=67043328
        ),
    )(
        item_lengths,
        layer_input,
        out_grad,
        patch_coords,
        w_qkv.reshape(width, 3 * hd).T,
        w_out,
        w_fc1,
        w_fc2,
        ln1_gain,
        ln1_shift,
        ln2_gain,
        ln2_shift,
        b_out,
        b_fc2,
        b_fc1,
        b_qv,
        sincos_rows(width),
    )
    layer_output, input_grad, g_fc2, g_fc1, g_wout, g_qkv, small = results
    return (
        layer_output,
        input_grad.astype(f32),
        small[0],
        small[1],
        g_qkv.astype(f32).reshape(width, 3, hd),
        small[9:11, :hd],
        g_wout.astype(f32),
        small[4],
        small[2],
        small[3],
        g_fc1.astype(f32),
        small[8, :ff],
        g_fc2.astype(f32),
        small[5],
    )


def solution(mesh):
    placed = (
        P("dp", None),
        P(None, "dp"),
        P("dp"),
        P("dp", None),
        P(),
        P(),
        P(None, None, "tensor"),
        P(None, "tensor"),
        P("tensor", None),
        P(),
        P(),
        P(),
        P(None, "tensor"),
        P("tensor"),
        P("tensor", None),
        P(),
    )
    return jax.shard_map(
        functools.partial(on_device, mesh.shape["dp"]),
        mesh=mesh,
        in_specs=placed,
        out_specs=(
            P("dp", None),
            P("dp", None),
            P(),
            P(),
            P(None, None, "tensor"),
            P(None, "tensor"),
            P("tensor", None),
            P(),
            P(),
            P(),
            P(None, "tensor"),
            P("tensor"),
            P("tensor", None),
            P(),
        ),
        check_vma=False,
    )
```

```python
import functools

import jax
import jax.numpy as jnp
import ml_dtypes
import numpy as np
from jax import lax
from jax.experimental import pallas as pl
from jax.experimental.pallas import tpu as pltpu
from jax.sharding import PartitionSpec as P

HEAD_DIM = 64
NORM_EPS = 1e-06
MASK_FILL = -1e30
LOG2E = 1.4426950408889634
BLK = 128
COORDS = 64
BEFORE_ATTENTION = ["wg2", "f2a", "f2b", "f2c", "mp", "wg1a", "f1a", "mf1", "wg1b", "f1b", "wg1c", "f1c", "vr", "f2a", "f2b", "n2b", "mla", "md0"]
IN_ATTENTION = (
    [["f2c", "f2a"], [], ["mf2", "f2c", "f1a", "md1", "f2a"]],
    [["lo0", "f1b", "f2c"], ["f2a", "f1a"], ["lo1", "f1b", "f2c", "f2b", "f1c", "md2", "gw", "w", "lo2", "f2a"]],
    [["f1a", "f1b"], ["of0", "f2c"], ["f2b", "w", "f1c"]],
)
AFTER_ATTENTION = ["fz", "of1", "f1a", "st0", "f2a", "f1b", "wqa", "qa", "st1", "f2b", "w", "na0", "of2", "wqb", "qb", "wqc", "qc", "f2c", "f1c", "st2", "na1", "f1a", "sums", "qa", "f1b", "na2", "f2b", "w", "nb0", "qb", "qc", "f1c", "nb1", "fo", "qa", "f1a", "nb2", "sm", "f2b", "sm", "f1b", "w", "if0", "qc", "qb", "f1c", "qa", "if1", "fi0", "w", "qc", "qb", "qa", "if2", "fi1", "f1c", "sm", "qc", "qb", "qa", "sm", "qc", "qb", "sm", "qa", "qc", "qb", "sm"]
f32 = jnp.float32
bf16 = jnp.bfloat16


def mm(a, b):
    return lax.dot_general(a, b, (((1,), (0,)), ((), ())), preferred_element_type=f32)


def mm_nt(a, b):
    return lax.dot_general(a, b, (((1,), (1,)), ((), ())), preferred_element_type=f32)


def mm_tn(a, b):
    return lax.dot_general(a, b, (((0,), (0,)), ((), ())), preferred_element_type=f32)


def norm_parts(v):
    width = v.shape[-1]
    mean = jnp.sum(v, axis=-1, keepdims=True) * (1.0 / width)
    centred = v - mean
    spread = jnp.sum(centred * centred, axis=-1, keepdims=True) * (1.0 / width)
    r = lax.rsqrt(spread + NORM_EPS)
    return centred * r, r


def norm_back(u, gain, x_hat, r):
    width = u.shape[-1]
    ug = u * gain
    m1 = jnp.sum(ug, axis=-1, keepdims=True) * (1.0 / width)
    m2 = jnp.sum(ug * x_hat, axis=-1, keepdims=True) * (1.0 / width)
    return r * (ug - m1 - x_hat * m2)


def gelu_pair(v):
    phi = 0.5 * (1.0 + lax.erf(v * 0.7071067811865476))
    dens = jnp.exp(-0.5 * v * v) * 0.3989422804014327
    return v * phi, phi + v * dens


class Sems:
    def __init__(self):
        self.count = 0
        self.ready_count = 0
        self.ready = None
        self.one = None
        self.send = None
        self.recv = None

    def take(self, n=1):
        first = self.count
        self.count += n
        return first


def remote(sems, idx, src, dst, target):
    return pltpu.make_async_remote_copy(
        src_ref=src,
        dst_ref=dst,
        send_sem=sems.send.at[idx],
        recv_sem=sems.recv.at[idx],
        device_id=target,
        device_id_type=pl.DeviceIdType.MESH,
    )


class Gather:
    def __init__(self, sems, parts, view, t):
        self.sems, self.view, self.t = sems, view, t
        self.base = sems.take(3 * parts)
        self.parts = parts
        self.sib = t + 1 - 2 * lax.rem(t, 2)
        self.opp = lax.rem(t + 2, 4)

    def copy(self, kind, s, owner):
        ref = self.view(s, owner)
        target = {"tensor": self.opp if kind == 1 else self.sib}
        return remote(self.sems, self.base + kind * self.parts + s, ref, ref, target)

    def start(self, s):
        self.copy(1, s, self.t).start()
        self.copy(0, s, self.t).start()

    def forward(self, s):
        self.copy(1, s, self.opp).wait_recv()
        self.copy(2, s, self.opp).start()

    def finish(self, s):
        self.copy(0, s, self.sib).wait_recv()
        self.copy(2, s, lax.rem(self.sib + 2, 4)).wait_recv()
        self.copy(0, s, self.t).wait_send()
        self.copy(1, s, self.t).wait_send()
        self.copy(2, s, self.opp).wait_send()


class Scatter:
    def __init__(self, sems, parts, bufs, t):
        self.part, self.got_a, self.got_b = bufs
        self.sems = sems
        self.base = sems.take(2 * parts)
        self.parts = parts
        self.core = lax.rem(t, 2)
        self.chip = t // 2
        self.sib = t + 1 - 2 * lax.rem(t, 2)
        self.opp = lax.rem(t + 2, 4)

    def store(self, s, value):
        for o in range(4):
            self.part[s, o % 2, o // 2] = value[o * BLK : (o + 1) * BLK].astype(bf16)

    def copy_a(self, s):
        return remote(
            self.sems, self.base + s, self.part.at[s, 1 - self.core], self.got_a.at[s], {"tensor": self.sib}
        )

    def copy_b(self, s):
        return remote(
            self.sems,
            self.base + self.parts + s,
            self.part.at[s, self.core, 1 - self.chip],
            self.got_b.at[s],
            {"tensor": self.opp},
        )

    def start(self, s):
        self.copy_a(s).start()

    def across(self, s):
        self.copy_a(s).wait()
        other = 1 - self.chip
        self.part[s, self.core, other] = (
            self.part[s, self.core, other].astype(f32) + self.got_a[s, other].astype(f32)
        ).astype(bf16)
        self.copy_b(s).start()

    def finish(self, s):
        self.copy_b(s).wait()
        return (
            self.part[s, self.core, self.chip].astype(f32)
            + self.got_a[s, self.chip].astype(f32)
            + self.got_b[s].astype(f32)
        )


class Reduce:
    def __init__(self, sems, ref, got, rows, cols, halvings, order, dp, log_n, first=0, spot=0):
        self.sems, self.ref, self.got, self.cols = sems, ref, got, cols
        rest = [b for b in range(log_n) if b not in order[:halvings]]
        self.bits = list(order[:halvings]) + rest
        self.halvings = halvings
        self.partners = [dp + (1 << b) * (1 - 2 * lax.rem(dp // (1 << b), 2)) for b in self.bits]
        self.base = sems.take(len(self.bits) + halvings)
        self.ready = sems.ready_count
        sems.ready_count += halvings
        self.low, self.size, self.spot = [first], [rows], []
        at = spot
        for j, b in enumerate(self.bits):
            side = lax.rem(dp // (1 << b), 2)
            if j < halvings:
                half = self.size[-1] // 2
                self.low.append(self.low[-1] + side * half)
                self.size.append(half)
            else:
                self.low.append(self.low[-1])
                self.size.append(self.size[-1])
            self.spot.append(at)
            at += self.size[-1]

    @staticmethod
    def got_rows(rows, halvings, log_n):
        return sum(rows >> (j + 1) for j in range(halvings)) + (log_n - halvings) * (rows >> halvings)

    def partner(self, j):
        return {"dp": self.partners[j]}

    def at(self, ref, low, size):
        if not isinstance(low, int):
            low = pl.multiple_of(low, 16)
        return ref.at[pl.ds(low, size), pl.ds(0, self.cols)]

    def copy_in(self, j):
        size = self.size[j + 1]
        if j < self.halvings:
            other = self.low[j] + self.low[j] + size - self.low[j + 1]
        else:
            other = self.low[j]
        return remote(
            self.sems,
            self.base + j,
            self.at(self.ref, other, size),
            self.at(self.got, self.spot[j], size),
            self.partner(j),
        )

    def copy_back(self, j):
        here = self.at(self.ref, self.low[j + 1], self.size[j + 1])
        return remote(self.sems, self.base + len(self.bits) + j, here, here, self.partner(j))

    def copy_home(self, j):
        size = self.size[j + 1]
        other = self.low[j] + self.low[j] + size - self.low[j + 1]
        here = self.at(self.ref, other, size)
        return remote(self.sems, self.base + len(self.bits) + j, here, here, self.partner(j))

    def begin(self, j):
        self.copy_in(j).start()

    def add(self, j):
        self.copy_in(j).wait()
        if j < self.halvings:
            pl.semaphore_signal(
                self.sems.ready.at[self.ready + j],
                inc=self.sems.one,
                device_id=self.partner(j),
                device_id_type=pl.DeviceIdType.MESH,
            )
        mine = self.at(self.ref, self.low[j + 1], self.size[j + 1])
        theirs = self.at(self.got, self.spot[j], self.size[j + 1])
        mine[...] = (mine[...].astype(f32) + theirs[...].astype(f32)).astype(bf16)

    def give(self, j):
        pl.semaphore_wait(self.sems.ready.at[self.ready + j], self.sems.one)
        self.copy_back(j).start()

    def take(self, j):
        self.copy_back(j).wait_send()
        self.copy_home(j).wait_recv()

    def steps(self):
        out = [lambda: self.begin(0)]
        n = len(self.bits)
        for j in range(n):

            def step(j=j):
                self.add(j)
                if j + 1 < n:
                    self.begin(j + 1)
                else:
                    self.give(self.halvings - 1)

            out.append(step)
        for j in reversed(range(self.halvings)):

            def back(j=j):
                self.take(j)
                if j > 0:
                    self.give(j - 1)

            out.append(back)
        return out


def layer_kernel(
    geo,
    lens,
    x_in,
    og_in,
    coords,
    w_qkv,
    w_out_in,
    w_fc1_in,
    w_fc2_in,
    v0,
    v1,
    v2,
    v3,
    v4,
    v5,
    v6,
    b_qv,
    tab3,
    act_ol,
    n2_oi,
    g_fc2,
    g_fc1,
    g_wout,
    g_qkv,
    out_small,
    x_mg,
    tg,
    n1,
    q_t,
    k_t,
    v_t,
    rows3,
    probs,
    mix,
    linv,
    w_out,
    w_fc1,
    w_fc2,
    mid_own,
    pg_dq,
    part0,
    got_a0,
    got_b0,
    part1,
    got_a1,
    got_b1,
    mg_own,
    delta,
    acc,
    r_fc2,
    r_fc1,
    r_wout,
    r_qkv,
    segk,
    small,
    small_got,
    fc1_sums,
    send,
    recv,
    ready,
    local,
):
    parts, log_n, heads = geo
    do_t = v_t
    vecs = (v0, v1, v2, v3, v4, v5, v6)
    size = 4 * BLK
    dp = lax.axis_index("dp")
    t = lax.axis_index("tensor")
    sib = t + 1 - 2 * lax.rem(t, 2)
    opp = lax.rem(t + 2, 4)
    width = x_mg.shape[1]
    hd = heads * HEAD_DIM

    sems = Sems()
    sems.send, sems.recv, sems.ready = send, recv, ready
    sems.one = lax.rem(t, 1) + 1

    def part_rows(s):
        return pl.ds(pl.multiple_of(s * size, size), size)

    def own_rows(s, owner):
        return pl.ds(pl.multiple_of(s * size + owner * BLK, BLK), BLK)

    def slot_rows(s, owner):
        return pl.ds(pl.multiple_of(owner * (parts * BLK) + s * BLK, BLK), BLK)

    ag_w = Gather(sems, 1, lambda s, o: w_out.at[pl.ds(pl.multiple_of(o * hd, hd), hd)], t)
    ag_mix = Gather(sems, parts, lambda s, o: mix.at[s, pl.ds(pl.multiple_of(o * hd, hd), hd)], t)
    ag_mg = Gather(sems, parts, lambda s, o: x_mg.at[own_rows(s, o)], t)
    ag_out = Gather(sems, parts, lambda s, o: act_ol.at[slot_rows(s, o)], t)
    ag_in = Gather(sems, parts, lambda s, o: n2_oi.at[slot_rows(s, o)], t)
    rs_n2 = Scatter(sems, parts, (part0, got_a0, got_b0), t)
    rs_mlp = Scatter(sems, parts, (part1, got_a1, got_b1), t)
    rs_n1 = Scatter(sems, parts, (part0, got_a0, got_b0), t)
    third = width // 3
    along_x, along_z = (0, 1, 2), (1, 0, 2)
    chains = {}

    def unit(name, ref, got, rows, cols, halvings, order, i=0):
        first, spot = i * rows, i * Reduce.got_rows(rows, halvings, log_n)
        total = Reduce(sems, ref, got, rows, cols, halvings, order, dp, log_n, first, spot)
        chains[name] = total.steps()

    for i in range(3):
        unit("f2" + "abc"[i], g_fc2, r_fc2, third, width, 3, along_z if i == 1 else along_x, i)
    for i in range(3):
        unit("f1" + "abc"[i], g_fc1, r_fc1, third, width, 3, along_x, i)
    unit("w", g_wout, r_wout, hd, width, 2, along_x[:2])
    for i in range(3):
        unit("q" + "abc"[i], g_qkv, r_qkv, third, 3 * hd, 3, along_z if i == 2 else along_x, i)
    small_base = sems.take(2 + log_n)

    n_local = [0]
    pending = []

    def fetch(src, dst):
        cp = pltpu.make_async_copy(src, dst, local.at[n_local[0]])
        n_local[0] += 1
        cp.start()
        return cp

    x_loads = [
        [fetch(x_in.at[slot_rows(s, o)], x_mg.at[own_rows(s, o)]) for o in range(4)] for s in range(parts)
    ]
    w_out_load = fetch(w_out_in, w_out.at[pl.ds(pl.multiple_of(t * hd, hd), hd)])
    fc1_load = fetch(w_fc1_in, w_fc1)
    fc2_load = fetch(w_fc2_in, w_fc2)
    tg_loads = [
        fetch(og_in.at[slot_rows(s, o)], tg.at[own_rows(s, o)]) for s in range(parts) for o in range(4)
    ]

    barrier = pltpu.get_barrier_semaphore()
    for target in (sib, opp):
        pl.semaphore_signal(
            barrier, inc=1, device_id={"tensor": target}, device_id_type=pl.DeviceIdType.MESH
        )
    for b in range(log_n):
        step = 1 << b
        other = dp + step * (1 - 2 * lax.rem(dp // step, 2))
        pl.semaphore_signal(
            barrier, inc=1, device_id={"dp": other}, device_id_type=pl.DeviceIdType.MESH
        )


    def row(ref):
        return ref[...].astype(f32).reshape(1, ref.shape[0])

    ln1_gain, ln1_shift, ln2_gain, ln2_shift, b_out, b_fc2, b_fc1 = [row(v) for v in vecs]
    b_q, b_v = b_qv[0:1, :].astype(f32), b_qv[1:2, :].astype(f32)

    ends, total = [], 0
    for i in range(lens.shape[0]):
        total = total + lens[i]
        ends.append(total)

    def segment_of(place):
        passed = jnp.zeros_like(place)
        for e in ends:
            passed = passed + jnp.where(place >= e, 1, 0)
        return jnp.where(place < ends[-1], passed, len(ends) + place)

    def positions(rows_of, c):
        n = c.shape[1]
        values = lax.broadcasted_iota(jnp.int32, (COORDS, n), 0)
        cols = []
        for i in range(3):
            hot = jnp.where(values == c[i : i + 1, :], 1.0, 0.0).astype(bf16)
            cols.append(mm_tn(jnp.concatenate([hot, hot, hot], axis=0), tab3[...]))
        return jnp.concatenate(cols, axis=1)

    def lane_blocks(ref, s):
        return jnp.concatenate([ref[:, slot_rows(s, o)] for o in range(4)], axis=1)

    def hidden_of(s):
        return x_mg[part_rows(s), :].astype(f32) + positions(None, lane_blocks(coords, s))

    for s in range(parts):
        for cp in x_loads[s]:
            cp.wait()

    def project(s, carry):
        for o in range(4):
            place = lax.broadcasted_iota(jnp.int32, (BLK, BLK), 0) + (o * parts * BLK + s * BLK)
            segk[own_rows(s, o), :] = segment_of(place)
        x_hat, _ = norm_parts(hidden_of(s))
        low = (x_hat * ln1_gain + ln1_shift).astype(bf16)
        n1[part_rows(s), :] = low
        proj = mm_nt(low, w_qkv[...])
        q = (proj[:, :hd] + b_q).astype(bf16).astype(f32).T.astype(bf16)
        k = proj[:, hd : 2 * hd].astype(bf16).astype(f32).T.astype(bf16)
        v = (proj[:, 2 * hd :] + b_v).astype(bf16).astype(f32).T.astype(bf16)
        for h in range(heads):
            head = slice(h * HEAD_DIM, (h + 1) * HEAD_DIM)
            q_t[h, :, part_rows(s)] = q[head]
            k_t[h, :, part_rows(s)] = k[head]
            v_t[h, :, part_rows(s)] = v[head]
            rows3[h, part_rows(s), :] = k[head].astype(f32).T.astype(bf16)

        @pl.when(s == 0)
        def _():
            pl.semaphore_wait(barrier, 2 + log_n)
            ag_w.start(0)

        return carry

    w_out_load.wait()
    lax.fori_loop(0, parts, project, 0)

    def attend(s, carry):
        place = jnp.concatenate(
            [
                lax.broadcasted_iota(jnp.int32, (1, BLK), 1) + (o * parts * BLK + s * BLK)
                for o in range(4)
            ],
            axis=1,
        )
        allowed = segk[...][:, :1] == segment_of(place)
        for h in range(heads):
            if h == heads - 1:

                @pl.when(s >= 2)
                def _():
                    ag_mix.forward(s - 2)

            scores = mm(rows3[h], q_t[h, :, part_rows(s)])
            scores = jnp.where(allowed, scores * (LOG2E / HEAD_DIM**0.5), MASK_FILL)
            top = jnp.max(scores, axis=0, keepdims=True)
            raised = jnp.exp2(scores - top)
            inv = 1.0 / jnp.sum(raised, axis=0, keepdims=True)
            low = raised.astype(bf16)
            probs[h, :, part_rows(s)] = low
            linv[h, :, part_rows(s)] = inv
            mixed = mm(v_t[h], low) * inv
            mix[s, pl.ds(pl.multiple_of(t * hd + h * HEAD_DIM, HEAD_DIM), HEAD_DIM), :] = mixed.astype(bf16)
        ag_mix.start(s)

        @pl.when(s == 1)
        def _():
            ag_w.forward(0)

        return carry

    lax.fori_loop(0, parts, attend, 0)
    for cp in tg_loads:
        cp.wait()
    fc1_load.wait()
    fc2_load.wait()
    ag_w.finish(0)
    fc1_sums[...] = jnp.zeros_like(fc1_sums)
    small[0] = jnp.zeros_like(small[0])

    def visible_rows(s, owner):
        return segk[own_rows(s, owner), :][:, :1] < len(ends)

    def second_norm_back(s):
        u = rs_n2.finish(s)
        middle = mid_own[s]
        x_hat, r = norm_parts(middle)
        grad = tg[own_rows(s, t), :].astype(f32) + norm_back(u, ln2_gain, x_hat, r)
        mg_own[s] = grad
        small[0, 2:3, :] += jnp.sum(u * x_hat, axis=0, keepdims=True)
        small[0, 3:4, :] += jnp.sum(u, axis=0, keepdims=True)
        small[0, 4:5, :] += jnp.sum(grad, axis=0, keepdims=True)
        small[0, 5:6, :] += jnp.sum(tg[own_rows(s, t), :].astype(f32), axis=0, keepdims=True)
        x_mg[own_rows(s, t), :] = grad.astype(bf16)
        ag_mg.start(s)

    def feed(s, carry):
        ag_mix.finish(s)
        attn = mm_tn(mix[s], w_out[...])
        middle = hidden_of(s) + attn + b_out
        mine = middle[:BLK]
        for o in range(1, 4):
            mine = jnp.where(t == o, middle[o * BLK : (o + 1) * BLK], mine)
        mid_own[s] = mine
        x_hat, _ = norm_parts(middle)
        low = (x_hat * ln2_gain + ln2_shift).astype(bf16)
        n2_oi[part_rows(s), :] = low
        value, slope = gelu_pair(mm(low, w_fc1[...]) + b_fc1)
        act_ol[part_rows(s), :] = value.astype(bf16)
        shown = segk[part_rows(s), :][:, :1] < len(ends)
        top = jnp.where(shown, tg[part_rows(s), :].astype(f32), 0.0).astype(bf16)
        tg[part_rows(s), :] = top
        pre = (mm_nt(top, w_fc2[...]) * slope).astype(bf16)
        pg_dq[part_rows(s), :] = pre
        fc1_sums[0:1, :] += jnp.sum(pre.astype(f32), axis=0, keepdims=True)
        @pl.when(s + 1 < parts)
        def _():
            ag_mix.forward(s + 1)

        rs_n2.store(s, mm_nt(pre, w_fc1[...]))
        rs_n2.start(s)

        @pl.when(s >= 1)
        def _():
            second_norm_back(s - 1)

        @pl.when(s >= 2)
        def _():
            ag_mg.forward(s - 2)

        rs_n2.across(s)
        return carry

    lax.fori_loop(0, parts, feed, 0)

    def weight_grad(dst, left, right, cols, first, last):
        for i in range(first, last):
            rows = slice(i * third, (i + 1) * third)
            dst[rows, :cols] = mm_tn(left[:, rows], right[:, :cols]).astype(bf16)

    own = pl.ds(pl.multiple_of(t * hd, hd), hd)
    x_own_loads = []

    def layer_out(s):
        total = mid_own[s] + rs_mlp.finish(s) + b_fc2
        act_ol[slot_rows(s, t), :] = jnp.where(visible_rows(s, t), total, 0.0).astype(bf16)
        ag_out.start(s)

    def mixed_grad(s):
        ag_mg.finish(s)
        rows = part_rows(s)
        low = mm_nt(x_mg[rows, :], w_out[own, :]).astype(bf16).astype(f32).T
        for h in range(heads):
            scaled = (low[h * HEAD_DIM : (h + 1) * HEAD_DIM] * linv[h, :, rows]).astype(bf16)
            do_t[h, :, rows] = scaled
            mixed = mix[s, pl.ds(pl.multiple_of(t * hd + h * HEAD_DIM, HEAD_DIM), HEAD_DIM), :]
            delta[h, :, rows] = jnp.sum(scaled.astype(f32) * mixed.astype(f32), axis=0, keepdims=True)

    def collect(s):
        rows = part_rows(s)
        for h in range(heads):
            low = do_t[h, :, rows].astype(f32).T.astype(bf16)
            pg_dq[rows, h * HEAD_DIM : (h + 1) * HEAD_DIM] = low
            key = acc[h, rows, HEAD_DIM:] * (1.0 / HEAD_DIM**0.5)
            pg_dq[rows, hd + h * HEAD_DIM : hd + (h + 1) * HEAD_DIM] = key.astype(bf16)
            pg_dq[rows, 2 * hd + h * HEAD_DIM : 2 * hd + (h + 1) * HEAD_DIM] = acc[h, rows, :HEAD_DIM].astype(bf16)

    def out_weight_grad():
        total = mm(mix[0, own, :], x_mg[part_rows(0), :])
        for s in range(1, parts):
            total = total + mm(mix[s, own, :], x_mg[part_rows(s), :])
        g_wout[...] = total.astype(bf16)

    def first_norm_back(s):
        if s == 0:
            for cp in x_own_loads:
                cp.wait()
        u = rs_n1.finish(s)
        hidden = tg[own_rows(s, t), :].astype(f32) + positions(None, coords[:, slot_rows(s, t)])
        x_hat, r = norm_parts(hidden)
        grad = mg_own[s] + norm_back(u, ln1_gain, x_hat, r)
        small[0, 0:1, :] += jnp.sum(u * x_hat, axis=0, keepdims=True)
        small[0, 1:2, :] += jnp.sum(u, axis=0, keepdims=True)
        n2_oi[slot_rows(s, t), :] = grad.astype(bf16)
        ag_in.start(s)

    def sums():
        total = jnp.sum(pg_dq[:, : 3 * hd].astype(f32), axis=0, keepdims=True)
        small[0, 8:9, :] = fc1_sums[0:1, :]
        small[0, 9:10, :hd] = total[:, :hd]
        small[0, 10:11, :hd] = total[:, 2 * hd :]

    hops = [(8, {"tensor": sib}), (8, {"tensor": opp})]
    for b in range(log_n):
        step = 1 << b
        hops.append((16, {"dp": dp + step * (1 - 2 * lax.rem(dp // step, 2))}))

    def small_copy(i):
        rows, target = hops[i]
        return remote(
            sems, small_base + i, small.at[i, pl.ds(0, rows)], small_got.at[i, pl.ds(0, rows)], target
        )

    def small_add(i):
        rows = hops[i][0]
        small_copy(i).wait()
        small[i + 1, 0:rows] = small[i, 0:rows] + small_got[i, 0:rows]
        if rows < 16:
            small[i + 1, rows:16] = small[i, rows:16]
        if i + 1 < len(hops):
            small_copy(i + 1).start()

    small_steps = [lambda: small_copy(0).start()] + [
        functools.partial(small_add, i) for i in range(len(hops))
    ]

    def do(token):
        kind, at = token[:2], token[2:]
        if token in chains:
            chains[token].pop(0)()
        elif token == "wg2":
            weight_grad(g_fc2, act_ol, tg, width, 0, 3)
        elif token == "mp":

            def product(s, carry):
                rs_mlp.store(s, mm(act_ol[part_rows(s), :], w_fc2[...]))
                rs_mlp.start(s)
                return carry

            lax.fori_loop(0, parts, product, 0)
        elif token == "vr":
            for h in range(heads):
                rows3[h] = v_t[h].astype(f32).T.astype(bf16)
        elif token == "n2b":
            second_norm_back(parts - 1)
            for s in range(parts):
                x_own_loads.append(fetch(x_in.at[slot_rows(s, t)], tg.at[own_rows(s, t)]))
        elif token == "mla":
            for s in range(parts):
                rs_mlp.across(s)
        elif kind == "wg":
            i = "abc".index(token[3])
            weight_grad(g_fc1, n2_oi, pg_dq, width, i, i + 1)
        elif kind == "mf":
            ag_mg.forward(int(at))
        elif kind == "md":
            mixed_grad(int(at))
        elif token == "gw":
            out_weight_grad()
        elif kind == "lo":
            layer_out(int(at))
        elif kind == "of":
            ag_out.forward(int(at))
        elif token == "fz":
            for s in range(parts):
                collect(s)
        elif kind == "st":
            s = int(at)
            rs_n1.store(s, mm(pg_dq[part_rows(s), : 3 * hd], w_qkv[...]))
            rs_n1.start(s)
        elif kind == "na":
            rs_n1.across(int(at))
        elif kind == "wq":
            i = "abc".index(at)
            weight_grad(g_qkv, n1, pg_dq, 3 * hd, i, i + 1)
        elif kind == "nb":
            first_norm_back(int(at))
        elif kind == "if":
            ag_in.forward(int(at))
        elif kind == "fi":
            ag_in.finish(int(at))
        elif token == "sums":
            sums()
        elif token == "sm":
            small_steps.pop(0)()
        elif token == "fo":
            for s in range(parts):
                ag_out.finish(s)

    def run(tokens):
        for token in tokens:
            do(token)

    run(BEFORE_ATTENTION)

    for s in range(parts):
        rows = part_rows(s)

        def back(h, carry, s=s, rows=rows):
            p = probs[h, :, rows]
            low = do_t[h, :, rows]
            wg = mm(rows3[h], low)
            sg = (p.astype(f32) * (wg - delta[h, :, rows])).astype(bf16)
            dv = mm(p, low.astype(f32).T.astype(bf16))
            dk = mm(sg, q_t[h, :, rows].astype(f32).T.astype(bf16))
            do_t[h, :, rows] = (mm(k_t[h], sg) * (1.0 / HEAD_DIM**0.5)).astype(bf16)
            if s == 0:
                acc[h, :, :HEAD_DIM] = dv
                acc[h, :, HEAD_DIM:] = dk
            else:
                acc[h, :, :HEAD_DIM] += dv
                acc[h, :, HEAD_DIM:] += dk
            for k in range(heads - 1):

                @pl.when(h == k)
                def _(k=k):
                    run(IN_ATTENTION[s][k])

            return carry

        lax.fori_loop(0, heads, back, 0)
        run(IN_ATTENTION[s][heads - 1])

    run(AFTER_ATTENTION)
    while small_steps or any(chains.values()):
        for name in ("qa", "qb", "qc", "f2a", "f2b", "f2c", "f1a", "f1b", "f1c", "w"):
            if chains[name]:
                do(name)
        if small_steps:
            do("sm")
    small_out = fetch(small.at[len(hops)], out_small)
    ag_in.finish(parts - 1)
    small_out.wait()


def sincos_rows(feature_count):
    half_width = feature_count // 6
    ladder = np.arange(half_width, dtype=np.float32) / np.float32(half_width)
    frequency = np.power(np.float32(10000.0), -ladder).astype(np.float32)
    angles = (np.arange(COORDS, dtype=np.float32)[:, None] * frequency[None, :]).astype(np.float32)
    wide = angles.astype(np.float64)
    left = np.concatenate([np.sin(wide), np.cos(wide)], axis=1)
    terms = []
    for _ in range(3):
        terms.append(left.astype(np.float32).astype(ml_dtypes.bfloat16))
        left = left - terms[-1].astype(np.float64)
    return jnp.asarray(np.concatenate(terms, axis=0))


def on_device(
    n_dp,
    layer_input,
    patch_coords,
    item_lengths,
    out_grad,
    ln1_gain,
    ln1_shift,
    w_qkv,
    b_qv,
    w_out,
    b_out,
    ln2_gain,
    ln2_shift,
    w_fc1,
    b_fc1,
    w_fc2,
    b_fc2,
):
    tokens, width = layer_input.shape
    hd = w_out.shape[0]
    ff = w_fc1.shape[1]
    heads = hd // HEAD_DIM
    parts = tokens // (4 * BLK)
    log_n = n_dp.bit_length() - 1
    size = 4 * BLK
    got = Reduce.got_rows
    vmem = lambda *s: pltpu.VMEM(s, bf16)
    vmem32 = lambda *s: pltpu.VMEM(s, f32)
    scratch = [
        vmem(tokens, width),
        vmem(tokens, width),
        vmem(tokens, width),
        vmem(heads, HEAD_DIM, tokens),
        vmem(heads, HEAD_DIM, tokens),
        vmem(heads, HEAD_DIM, tokens),
        vmem(heads, tokens, HEAD_DIM),
        vmem(heads, tokens, tokens),
        vmem(parts, 4 * hd, size),
        vmem32(heads, 1, tokens),
        vmem(4 * hd, width),
        vmem(width, ff),
        vmem(ff, width),
        vmem32(parts, BLK, width),
        vmem(tokens, width),
    ]
    for _ in range(2):
        scratch += [
            vmem(parts, 2, 2, BLK, width),
            vmem(parts, 2, BLK, width),
            vmem(parts, BLK, width),
        ]
    scratch += [
        vmem32(parts, BLK, width),
        vmem32(heads, 1, tokens),
        vmem32(heads, tokens, 2 * HEAD_DIM),
        vmem(3 * got(width // 3, 3, log_n), width),
        vmem(3 * got(width // 3, 3, log_n), width),
        vmem(got(hd, 2, log_n), width),
        vmem(3 * got(width // 3, 3, log_n), 3 * hd),
        pltpu.VMEM((tokens, BLK), jnp.int32),
        vmem32(3 + log_n, 16, width),
        vmem32(2 + log_n, 16, width),
        vmem32(8, ff),
    ]
    n_sems = 3 + 4 * 3 * parts + 3 * 2 * parts + 9 * (log_n + 3) + (log_n + 2) + 2 + log_n
    scratch += [
        pltpu.SemaphoreType.DMA((n_sems,)),
        pltpu.SemaphoreType.DMA((n_sems,)),
        pltpu.SemaphoreType.REGULAR((29,)),
        pltpu.SemaphoreType.DMA((4 * parts * 2 + parts + 3 + 10 + 2 + 4 * parts,)),
    ]
    hbm = pl.BlockSpec(memory_space=pl.ANY)
    here = pl.BlockSpec(memory_space=pltpu.VMEM)
    results = pl.pallas_call(
        functools.partial(layer_kernel, (parts, log_n, heads)),
        name="layer",
        out_shape=(
            vmem(tokens, width),
            vmem(tokens, width),
            vmem(ff, width),
            vmem(width, ff),
            vmem(hd, width),
            vmem(width, 3 * hd),
            jax.ShapeDtypeStruct((16, width), f32),
        ),
        in_specs=[pl.BlockSpec(memory_space=pltpu.SMEM), hbm, hbm, here, here, hbm, hbm, hbm] + [here] * 9,
        out_specs=(here,) * 6 + (hbm,),
        scratch_shapes=scratch,
        compiler_params=pltpu.CompilerParams(
            collective_id=0, has_side_effects=True, vmem_limit_bytes=67043328 - 2 * (2 * tokens * width + 2 * ff * width + 4 * hd * width) - 600000
        ),
    )(
        item_lengths,
        layer_input,
        out_grad,
        patch_coords,
        w_qkv.reshape(width, 3 * hd).T,
        w_out,
        w_fc1,
        w_fc2,
        ln1_gain,
        ln1_shift,
        ln2_gain,
        ln2_shift,
        b_out,
        b_fc2,
        b_fc1,
        b_qv,
        sincos_rows(width),
    )
    layer_output, input_grad, g_fc2, g_fc1, g_wout, g_qkv, small = results
    return (
        layer_output,
        input_grad.astype(f32),
        small[0],
        small[1],
        g_qkv.astype(f32).reshape(width, 3, hd),
        small[9:11, :hd],
        g_wout.astype(f32),
        small[4],
        small[2],
        small[3],
        g_fc1.astype(f32),
        small[8, :ff],
        g_fc2.astype(f32),
        small[5],
    )


def solution(mesh):
    placed = (
        P("dp", None),
        P(None, "dp"),
        P("dp"),
        P("dp", None),
        P(),
        P(),
        P(None, None, "tensor"),
        P(None, "tensor"),
        P("tensor", None),
        P(),
        P(),
        P(),
        P(None, "tensor"),
        P("tensor"),
        P("tensor", None),
        P(),
    )
    return jax.shard_map(
        functools.partial(on_device, mesh.shape["dp"]),
        mesh=mesh,
        in_specs=placed,
        out_specs=(
            P("dp", None),
            P("dp", None),
            P(),
            P(),
            P(None, None, "tensor"),
            P(None, "tensor"),
            P("tensor", None),
            P(),
            P(),
            P(),
            P(None, "tensor"),
            P("tensor"),
            P("tensor", None),
            P(),
        ),
        check_vma=False,
    )
```

```python
import functools

import jax
import jax.numpy as jnp
import ml_dtypes
import numpy as np
from jax import lax
from jax.experimental import pallas as pl
from jax.experimental.pallas import tpu as pltpu
from jax.sharding import PartitionSpec as P

HEAD_DIM = 64
NORM_EPS = 1e-06
MASK_FILL = -1e30
LOG2E = 1.4426950408889634
BLK = 128
COORDS = 64
BEFORE_ATTENTION = ["wg2", "f2a", "f2b", "f2c", "mp", "wg1a", "f1a", "mf1", "wg1b", "f1b", "wg1c", "f1c", "vr", "f2a", "f2b", "n2b", "mla", "md0"]
IN_ATTENTION = (
    [["f2c", "f2a"], [], ["mf2", "f2c", "f1a", "md1", "f2a"]],
    [["lo0", "f1b", "f2c"], ["f2a", "f1a"], ["lo1", "f1b", "f2c", "f2b", "f1c", "md2", "gw", "w", "lo2", "f2a"]],
    [["f1a", "f1b"], ["of0", "f2c"], ["f2b", "w", "f1c"]],
)
AFTER_ATTENTION = ["fz", "of1", "f1a", "st0", "f2a", "f1b", "wqa", "qa", "st1", "f2b", "w", "na0", "of2", "wqb", "qb", "wqc", "qc", "f2c", "f1c", "st2", "na1", "f1a", "sums", "qa", "f1b", "na2", "f2b", "w", "nb0", "qb", "qc", "f1c", "nb1", "fo", "qa", "f1a", "nb2", "sm", "f2b", "sm", "f1b", "w", "if0", "qc", "qb", "f1c", "qa", "if1", "fi0", "w", "qc", "qb", "qa", "if2", "fi1", "f1c", "sm", "qc", "qb", "qa", "sm", "qc", "qb", "sm", "qa", "qc", "qb", "sm"]
f32 = jnp.float32
bf16 = jnp.bfloat16


def mm(a, b):
    return lax.dot_general(a, b, (((1,), (0,)), ((), ())), preferred_element_type=f32)


def mm_nt(a, b):
    return lax.dot_general(a, b, (((1,), (1,)), ((), ())), preferred_element_type=f32)


def mm_tn(a, b):
    return lax.dot_general(a, b, (((0,), (0,)), ((), ())), preferred_element_type=f32)


def norm_parts(v):
    width = v.shape[-1]
    mean = jnp.sum(v, axis=-1, keepdims=True) * (1.0 / width)
    centred = v - mean
    spread = jnp.sum(centred * centred, axis=-1, keepdims=True) * (1.0 / width)
    r = lax.rsqrt(spread + NORM_EPS)
    return centred * r, r


def norm_back(u, gain, x_hat, r):
    width = u.shape[-1]
    ug = u * gain
    m1 = jnp.sum(ug, axis=-1, keepdims=True) * (1.0 / width)
    m2 = jnp.sum(ug * x_hat, axis=-1, keepdims=True) * (1.0 / width)
    return r * (ug - m1 - x_hat * m2)


def gelu_pair(v):
    phi = 0.5 * (1.0 + lax.erf(v * 0.7071067811865476))
    dens = jnp.exp(-0.5 * v * v) * 0.3989422804014327
    return v * phi, phi + v * dens


class Sems:
    def __init__(self):
        self.count = 0
        self.ready_count = 0
        self.ready = None
        self.one = None
        self.send = None
        self.recv = None

    def take(self, n=1):
        first = self.count
        self.count += n
        return first


def remote(sems, idx, src, dst, target):
    return pltpu.make_async_remote_copy(
        src_ref=src,
        dst_ref=dst,
        send_sem=sems.send.at[idx],
        recv_sem=sems.recv.at[idx],
        device_id=target,
        device_id_type=pl.DeviceIdType.MESH,
    )


class Gather:
    def __init__(self, sems, parts, view, t):
        self.sems, self.view, self.t = sems, view, t
        self.base = sems.take(3 * parts)
        self.parts = parts
        self.sib = t + 1 - 2 * lax.rem(t, 2)
        self.opp = lax.rem(t + 2, 4)

    def copy(self, kind, s, owner):
        ref = self.view(s, owner)
        target = {"tensor": self.opp if kind == 1 else self.sib}
        return remote(self.sems, self.base + kind * self.parts + s, ref, ref, target)

    def start(self, s):
        self.copy(1, s, self.t).start()
        self.copy(0, s, self.t).start()

    def forward(self, s):
        self.copy(1, s, self.opp).wait_recv()
        self.copy(2, s, self.opp).start()

    def finish(self, s):
        self.copy(0, s, self.sib).wait_recv()
        self.copy(2, s, lax.rem(self.sib + 2, 4)).wait_recv()
        self.copy(0, s, self.t).wait_send()
        self.copy(1, s, self.t).wait_send()
        self.copy(2, s, self.opp).wait_send()


class Scatter:
    def __init__(self, sems, parts, bufs, t):
        self.part, self.got_a, self.got_b = bufs
        self.sems = sems
        self.base = sems.take(2 * parts)
        self.parts = parts
        self.core = lax.rem(t, 2)
        self.chip = t // 2
        self.sib = t + 1 - 2 * lax.rem(t, 2)
        self.opp = lax.rem(t + 2, 4)

    def store(self, s, value):
        for o in range(4):
            self.part[s, o % 2, o // 2] = value[o * BLK : (o + 1) * BLK].astype(bf16)

    def copy_a(self, s):
        return remote(
            self.sems, self.base + s, self.part.at[s, 1 - self.core], self.got_a.at[s], {"tensor": self.sib}
        )

    def copy_b(self, s):
        return remote(
            self.sems,
            self.base + self.parts + s,
            self.part.at[s, self.core, 1 - self.chip],
            self.got_b.at[s],
            {"tensor": self.opp},
        )

    def start(self, s):
        self.copy_a(s).start()

    def across(self, s):
        self.copy_a(s).wait()
        other = 1 - self.chip
        self.part[s, self.core, other] = (
            self.part[s, self.core, other].astype(f32) + self.got_a[s, other].astype(f32)
        ).astype(bf16)
        self.copy_b(s).start()

    def finish(self, s):
        self.copy_b(s).wait()
        return (
            self.part[s, self.core, self.chip].astype(f32)
            + self.got_a[s, self.chip].astype(f32)
            + self.got_b[s].astype(f32)
        )


class Reduce:
    def __init__(self, sems, ref, got, rows, cols, halvings, order, dp, log_n, first=0, spot=0):
        self.sems, self.ref, self.got, self.cols = sems, ref, got, cols
        rest = [b for b in range(log_n) if b not in order[:halvings]]
        self.bits = list(order[:halvings]) + rest
        self.halvings = halvings
        self.partners = [dp + (1 << b) * (1 - 2 * lax.rem(dp // (1 << b), 2)) for b in self.bits]
        self.base = sems.take(len(self.bits) + halvings)
        self.ready = sems.ready_count
        sems.ready_count += halvings
        self.low, self.size, self.spot = [first], [rows], []
        at = spot
        for j, b in enumerate(self.bits):
            side = lax.rem(dp // (1 << b), 2)
            if j < halvings:
                half = self.size[-1] // 2
                self.low.append(self.low[-1] + side * half)
                self.size.append(half)
            else:
                self.low.append(self.low[-1])
                self.size.append(self.size[-1])
            self.spot.append(at)
            at += self.size[-1]

    @staticmethod
    def got_rows(rows, halvings, log_n):
        return sum(rows >> (j + 1) for j in range(halvings)) + (log_n - halvings) * (rows >> halvings)

    def partner(self, j):
        return {"dp": self.partners[j]}

    def at(self, ref, low, size):
        if not isinstance(low, int):
            low = pl.multiple_of(low, 16)
        return ref.at[pl.ds(low, size), pl.ds(0, self.cols)]

    def copy_in(self, j):
        size = self.size[j + 1]
        if j < self.halvings:
            other = self.low[j] + self.low[j] + size - self.low[j + 1]
        else:
            other = self.low[j]
        return remote(
            self.sems,
            self.base + j,
            self.at(self.ref, other, size),
            self.at(self.got, self.spot[j], size),
            self.partner(j),
        )

    def copy_back(self, j):
        here = self.at(self.ref, self.low[j + 1], self.size[j + 1])
        return remote(self.sems, self.base + len(self.bits) + j, here, here, self.partner(j))

    def copy_home(self, j):
        size = self.size[j + 1]
        other = self.low[j] + self.low[j] + size - self.low[j + 1]
        here = self.at(self.ref, other, size)
        return remote(self.sems, self.base + len(self.bits) + j, here, here, self.partner(j))

    def begin(self, j):
        self.copy_in(j).start()

    def add(self, j):
        self.copy_in(j).wait()
        if j < self.halvings:
            pl.semaphore_signal(
                self.sems.ready.at[self.ready + j],
                inc=self.sems.one,
                device_id=self.partner(j),
                device_id_type=pl.DeviceIdType.MESH,
            )
        mine = self.at(self.ref, self.low[j + 1], self.size[j + 1])
        theirs = self.at(self.got, self.spot[j], self.size[j + 1])
        mine[...] = (mine[...].astype(f32) + theirs[...].astype(f32)).astype(bf16)

    def give(self, j):
        pl.semaphore_wait(self.sems.ready.at[self.ready + j], self.sems.one)
        self.copy_back(j).start()

    def take(self, j):
        self.copy_back(j).wait_send()
        self.copy_home(j).wait_recv()

    def steps(self):
        out = [lambda: self.begin(0)]
        n = len(self.bits)
        for j in range(n):

            def step(j=j):
                self.add(j)
                if j + 1 < n:
                    self.begin(j + 1)
                else:
                    self.give(self.halvings - 1)

            out.append(step)
        for j in reversed(range(self.halvings)):

            def back(j=j):
                self.take(j)
                if j > 0:
                    self.give(j - 1)

            out.append(back)
        return out


def layer_kernel(
    geo,
    lens,
    x_in,
    og_in,
    coords,
    w_qkv,
    w_out_in,
    w_fc1_in,
    w_fc2_in,
    v0,
    v1,
    v2,
    v3,
    v4,
    v5,
    v6,
    b_qv,
    tab3,
    act_ol,
    n2_oi,
    g_fc2,
    g_fc1,
    g_wout,
    g_qkv,
    out_small,
    x_mg,
    tg,
    n1,
    q_t,
    k_t,
    v_t,
    rows3,
    probs,
    mix,
    linv,
    w_out,
    w_fc1,
    w_fc2,
    mid_own,
    pg_dq,
    part0,
    got_a0,
    got_b0,
    part1,
    got_a1,
    got_b1,
    mg_own,
    delta,
    acc,
    r_fc2,
    r_fc1,
    r_wout,
    r_qkv,
    segk,
    small,
    small_got,
    fc1_sums,
    send,
    recv,
    ready,
    local,
):
    parts, log_n, heads = geo
    do_t = v_t
    vecs = (v0, v1, v2, v3, v4, v5, v6)
    size = 4 * BLK
    dp = lax.axis_index("dp")
    t = lax.axis_index("tensor")
    sib = t + 1 - 2 * lax.rem(t, 2)
    opp = lax.rem(t + 2, 4)
    width = x_mg.shape[1]
    hd = heads * HEAD_DIM

    sems = Sems()
    sems.send, sems.recv, sems.ready = send, recv, ready
    sems.one = lax.rem(t, 1) + 1

    def part_rows(s):
        return pl.ds(pl.multiple_of(s * size, size), size)

    def own_rows(s, owner):
        return pl.ds(pl.multiple_of(s * size + owner * BLK, BLK), BLK)

    def slot_rows(s, owner):
        return pl.ds(pl.multiple_of(owner * (parts * BLK) + s * BLK, BLK), BLK)

    ag_w = Gather(sems, 1, lambda s, o: w_out.at[pl.ds(pl.multiple_of(o * hd, hd), hd)], t)
    ag_mix = Gather(sems, parts, lambda s, o: mix.at[s, pl.ds(pl.multiple_of(o * hd, hd), hd)], t)
    ag_mg = Gather(sems, parts, lambda s, o: x_mg.at[own_rows(s, o)], t)
    ag_out = Gather(sems, parts, lambda s, o: act_ol.at[slot_rows(s, o)], t)
    ag_in = Gather(sems, parts, lambda s, o: n2_oi.at[slot_rows(s, o)], t)
    rs_n2 = Scatter(sems, parts, (part0, got_a0, got_b0), t)
    rs_mlp = Scatter(sems, parts, (part1, got_a1, got_b1), t)
    rs_n1 = Scatter(sems, parts, (part0, got_a0, got_b0), t)
    third = width // 3
    along_x, along_z = (0, 1, 2), (1, 0, 2)
    chains = {}

    def unit(name, ref, got, rows, cols, halvings, order, i=0):
        first, spot = i * rows, i * Reduce.got_rows(rows, halvings, log_n)
        total = Reduce(sems, ref, got, rows, cols, halvings, order, dp, log_n, first, spot)
        chains[name] = total.steps()

    for i in range(3):
        unit("f2" + "abc"[i], g_fc2, r_fc2, third, width, 3, along_z if i == 1 else along_x, i)
    for i in range(3):
        unit("f1" + "abc"[i], g_fc1, r_fc1, third, width, 3, along_x, i)
    unit("w", g_wout, r_wout, hd, width, 2, along_x[:2])
    for i in range(3):
        unit("q" + "abc"[i], g_qkv, r_qkv, third, 3 * hd, 3, along_z if i == 2 else along_x, i)
    small_base = sems.take(2 + log_n)

    n_local = [0]
    pending = []

    def fetch(src, dst):
        cp = pltpu.make_async_copy(src, dst, local.at[n_local[0]])
        n_local[0] += 1
        cp.start()
        return cp

    x_loads = [
        [fetch(x_in.at[slot_rows(s, o)], x_mg.at[own_rows(s, o)]) for o in range(4)] for s in range(parts)
    ]
    w_out_load = fetch(w_out_in, w_out.at[pl.ds(pl.multiple_of(t * hd, hd), hd)])
    fc1_load = fetch(w_fc1_in, w_fc1)
    fc2_load = fetch(w_fc2_in, w_fc2)
    tg_loads = [
        fetch(og_in.at[slot_rows(s, o)], tg.at[own_rows(s, o)]) for s in range(parts) for o in range(4)
    ]

    barrier = pltpu.get_barrier_semaphore()
    for target in (sib, opp):
        pl.semaphore_signal(
            barrier, inc=1, device_id={"tensor": target}, device_id_type=pl.DeviceIdType.MESH
        )
    for b in range(log_n):
        step = 1 << b
        other = dp + step * (1 - 2 * lax.rem(dp // step, 2))
        pl.semaphore_signal(
            barrier, inc=1, device_id={"dp": other}, device_id_type=pl.DeviceIdType.MESH
        )


    def row(ref):
        return ref[...].astype(f32).reshape(1, ref.shape[0])

    ln1_gain, ln1_shift, ln2_gain, ln2_shift, b_out, b_fc2, b_fc1 = [row(v) for v in vecs]
    b_q, b_v = b_qv[0:1, :].astype(f32), b_qv[1:2, :].astype(f32)

    ends, total = [], 0
    for i in range(lens.shape[0]):
        total = total + lens[i]
        ends.append(total)

    def segment_of(place):
        passed = jnp.zeros_like(place)
        for e in ends:
            passed = passed + jnp.where(place >= e, 1, 0)
        return jnp.where(place < ends[-1], passed, len(ends) + place)

    def positions(rows_of, c):
        n = c.shape[1]
        values = lax.broadcasted_iota(jnp.int32, (COORDS, n), 0)
        cols = []
        for i in range(3):
            hot = jnp.where(values == c[i : i + 1, :], 1.0, 0.0).astype(bf16)
            cols.append(mm_tn(jnp.concatenate([hot, hot, hot], axis=0), tab3[...]))
        return jnp.concatenate(cols, axis=1)

    def lane_blocks(ref, s):
        return jnp.concatenate([ref[:, slot_rows(s, o)] for o in range(4)], axis=1)

    def hidden_of(s):
        return x_mg[part_rows(s), :].astype(f32) + positions(None, lane_blocks(coords, s))

    for s in range(parts):
        for cp in x_loads[s]:
            cp.wait()

    def project(s, carry):
        for o in range(4):
            place = lax.broadcasted_iota(jnp.int32, (BLK, BLK), 0) + (o * parts * BLK + s * BLK)
            segk[own_rows(s, o), :] = segment_of(place)
        x_hat, _ = norm_parts(hidden_of(s))
        low = (x_hat * ln1_gain + ln1_shift).astype(bf16)
        n1[part_rows(s), :] = low
        proj = mm_nt(low, w_qkv[...])
        q = (proj[:, :hd] + b_q).astype(bf16).astype(f32).T.astype(bf16)
        k = proj[:, hd : 2 * hd].astype(bf16).astype(f32).T.astype(bf16)
        v = (proj[:, 2 * hd :] + b_v).astype(bf16).astype(f32).T.astype(bf16)
        for h in range(heads):
            head = slice(h * HEAD_DIM, (h + 1) * HEAD_DIM)
            q_t[h, :, part_rows(s)] = q[head]
            k_t[h, :, part_rows(s)] = k[head]
            v_t[h, :, part_rows(s)] = v[head]
            rows3[h, part_rows(s), :] = k[head].astype(f32).T.astype(bf16)

        @pl.when(s == 0)
        def _():
            pl.semaphore_wait(barrier, 2 + log_n)
            ag_w.start(0)

        return carry

    w_out_load.wait()
    lax.fori_loop(0, parts, project, 0)

    def attend(s, carry):
        place = jnp.concatenate(
            [
                lax.broadcasted_iota(jnp.int32, (1, BLK), 1) + (o * parts * BLK + s * BLK)
                for o in range(4)
            ],
            axis=1,
        )
        allowed = segk[...][:, :1] == segment_of(place)
        for h in range(heads):
            if h == heads - 1:

                @pl.when(s >= 2)
                def _():
                    ag_mix.forward(s - 2)

            scores = mm(rows3[h], q_t[h, :, part_rows(s)])
            scores = jnp.where(allowed, scores * (LOG2E / HEAD_DIM**0.5), MASK_FILL)
            top = jnp.max(scores, axis=0, keepdims=True)
            raised = jnp.exp2(scores - top)
            inv = 1.0 / jnp.sum(raised, axis=0, keepdims=True)
            low = raised.astype(bf16)
            probs[h, :, part_rows(s)] = low
            linv[h, :, part_rows(s)] = inv
            mixed = mm(v_t[h], low) * inv
            mix[s, pl.ds(pl.multiple_of(t * hd + h * HEAD_DIM, HEAD_DIM), HEAD_DIM), :] = mixed.astype(bf16)
        ag_mix.start(s)

        @pl.when(s == 1)
        def _():
            ag_w.forward(0)

        return carry

    lax.fori_loop(0, parts, attend, 0)
    for cp in tg_loads:
        cp.wait()
    fc1_load.wait()
    fc2_load.wait()
    ag_w.finish(0)
    fc1_sums[...] = jnp.zeros_like(fc1_sums)
    small[0] = jnp.zeros_like(small[0])

    def visible_rows(s, owner):
        return segk[own_rows(s, owner), :][:, :1] < len(ends)

    def second_norm_back(s):
        u = rs_n2.finish(s)
        middle = mid_own[s]
        x_hat, r = norm_parts(middle)
        grad = tg[own_rows(s, t), :].astype(f32) + norm_back(u, ln2_gain, x_hat, r)
        mg_own[s] = grad
        small[0, 2:3, :] += jnp.sum(u * x_hat, axis=0, keepdims=True)
        small[0, 3:4, :] += jnp.sum(u, axis=0, keepdims=True)
        small[0, 4:5, :] += jnp.sum(grad, axis=0, keepdims=True)
        small[0, 5:6, :] += jnp.sum(tg[own_rows(s, t), :].astype(f32), axis=0, keepdims=True)
        x_mg[own_rows(s, t), :] = grad.astype(bf16)
        ag_mg.start(s)

    def feed(s, carry):
        ag_mix.finish(s)
        attn = mm_tn(mix[s], w_out[...])
        middle = hidden_of(s) + attn + b_out
        mine = middle[:BLK]
        for o in range(1, 4):
            mine = jnp.where(t == o, middle[o * BLK : (o + 1) * BLK], mine)
        mid_own[s] = mine
        x_hat, _ = norm_parts(middle)
        low = (x_hat * ln2_gain + ln2_shift).astype(bf16)
        n2_oi[part_rows(s), :] = low
        value, slope = gelu_pair(mm(low, w_fc1[...]) + b_fc1)
        act_ol[part_rows(s), :] = value.astype(bf16)
        shown = segk[part_rows(s), :][:, :1] < len(ends)
        top = jnp.where(shown, tg[part_rows(s), :].astype(f32), 0.0).astype(bf16)
        tg[part_rows(s), :] = top
        pre = (mm_nt(top, w_fc2[...]) * slope).astype(bf16)
        pg_dq[part_rows(s), :] = pre
        fc1_sums[0:1, :] += jnp.sum(pre.astype(f32), axis=0, keepdims=True)
        @pl.when(s + 1 < parts)
        def _():
            ag_mix.forward(s + 1)

        rs_n2.store(s, mm_nt(pre, w_fc1[...]))
        rs_n2.start(s)

        @pl.when(s >= 1)
        def _():
            second_norm_back(s - 1)

        @pl.when(s >= 2)
        def _():
            ag_mg.forward(s - 2)

        rs_n2.across(s)
        return carry

    lax.fori_loop(0, parts, feed, 0)

    def weight_grad(dst, left, right, cols, first, last):
        for i in range(first, last):
            rows = slice(i * third, (i + 1) * third)
            dst[rows, :cols] = mm_tn(left[:, rows], right[:, :cols]).astype(bf16)

    own = pl.ds(pl.multiple_of(t * hd, hd), hd)
    x_own_loads = []

    def layer_out(s):
        total = mid_own[s] + rs_mlp.finish(s) + b_fc2
        act_ol[slot_rows(s, t), :] = jnp.where(visible_rows(s, t), total, 0.0).astype(bf16)
        ag_out.start(s)

    def mixed_grad(s):
        ag_mg.finish(s)
        rows = part_rows(s)
        low = mm_nt(x_mg[rows, :], w_out[own, :]).astype(bf16).astype(f32).T
        for h in range(heads):
            scaled = (low[h * HEAD_DIM : (h + 1) * HEAD_DIM] * linv[h, :, rows]).astype(bf16)
            do_t[h, :, rows] = scaled
            mixed = mix[s, pl.ds(pl.multiple_of(t * hd + h * HEAD_DIM, HEAD_DIM), HEAD_DIM), :]
            delta[h, :, rows] = jnp.sum(scaled.astype(f32) * mixed.astype(f32), axis=0, keepdims=True)

    def collect(s):
        rows = part_rows(s)
        for h in range(heads):
            low = do_t[h, :, rows].astype(f32).T.astype(bf16)
            pg_dq[rows, h * HEAD_DIM : (h + 1) * HEAD_DIM] = low
            key = acc[h, rows, HEAD_DIM:] * (1.0 / HEAD_DIM**0.5)
            pg_dq[rows, hd + h * HEAD_DIM : hd + (h + 1) * HEAD_DIM] = key.astype(bf16)
            pg_dq[rows, 2 * hd + h * HEAD_DIM : 2 * hd + (h + 1) * HEAD_DIM] = acc[h, rows, :HEAD_DIM].astype(bf16)

    def out_weight_grad():
        total = mm(mix[0, own, :], x_mg[part_rows(0), :])
        for s in range(1, parts):
            total = total + mm(mix[s, own, :], x_mg[part_rows(s), :])
        g_wout[...] = total.astype(bf16)

    def first_norm_back(s):
        if s == 0:
            for cp in x_own_loads:
                cp.wait()
        u = rs_n1.finish(s)
        hidden = tg[own_rows(s, t), :].astype(f32) + positions(None, coords[:, slot_rows(s, t)])
        x_hat, r = norm_parts(hidden)
        grad = mg_own[s] + norm_back(u, ln1_gain, x_hat, r)
        small[0, 0:1, :] += jnp.sum(u * x_hat, axis=0, keepdims=True)
        small[0, 1:2, :] += jnp.sum(u, axis=0, keepdims=True)
        n2_oi[slot_rows(s, t), :] = grad.astype(bf16)
        ag_in.start(s)

    def sums():
        total = jnp.sum(pg_dq[:, : 3 * hd].astype(f32), axis=0, keepdims=True)
        small[0, 8:9, :] = fc1_sums[0:1, :]
        small[0, 9:10, :hd] = total[:, :hd]
        small[0, 10:11, :hd] = total[:, 2 * hd :]

    hops = [(8, {"tensor": sib}), (8, {"tensor": opp})]
    for b in range(log_n):
        step = 1 << b
        hops.append((16, {"dp": dp + step * (1 - 2 * lax.rem(dp // step, 2))}))

    def small_copy(i):
        rows, target = hops[i]
        return remote(
            sems, small_base + i, small.at[i, pl.ds(0, rows)], small_got.at[i, pl.ds(0, rows)], target
        )

    def small_add(i):
        rows = hops[i][0]
        small_copy(i).wait()
        if i + 1 == len(hops):
            out_small[...] = small[i] + small_got[i]
            return
        small[i + 1, 0:rows] = small[i, 0:rows] + small_got[i, 0:rows]
        if rows < 16:
            small[i + 1, rows:16] = small[i, rows:16]
        small_copy(i + 1).start()

    small_steps = [lambda: small_copy(0).start()] + [
        functools.partial(small_add, i) for i in range(len(hops))
    ]

    def do(token):
        kind, at = token[:2], token[2:]
        if token in chains:
            chains[token].pop(0)()
        elif token == "wg2":
            weight_grad(g_fc2, act_ol, tg, width, 0, 3)
        elif token == "mp":

            def product(s, carry):
                rs_mlp.store(s, mm(act_ol[part_rows(s), :], w_fc2[...]))
                rs_mlp.start(s)
                return carry

            lax.fori_loop(0, parts, product, 0)
        elif token == "vr":
            for h in range(heads):
                rows3[h] = v_t[h].astype(f32).T.astype(bf16)
        elif token == "n2b":
            second_norm_back(parts - 1)
            for s in range(parts):
                x_own_loads.append(fetch(x_in.at[slot_rows(s, t)], tg.at[own_rows(s, t)]))
        elif token == "mla":
            for s in range(parts):
                rs_mlp.across(s)
        elif kind == "wg":
            i = "abc".index(token[3])
            weight_grad(g_fc1, n2_oi, pg_dq, width, i, i + 1)
        elif kind == "mf":
            ag_mg.forward(int(at))
        elif kind == "md":
            mixed_grad(int(at))
        elif token == "gw":
            out_weight_grad()
        elif kind == "lo":
            layer_out(int(at))
        elif kind == "of":
            ag_out.forward(int(at))
        elif token == "fz":
            for s in range(parts):
                collect(s)
        elif kind == "st":
            s = int(at)
            rs_n1.store(s, mm(pg_dq[part_rows(s), : 3 * hd], w_qkv[...]))
            rs_n1.start(s)
        elif kind == "na":
            rs_n1.across(int(at))
        elif kind == "wq":
            i = "abc".index(at)
            weight_grad(g_qkv, n1, pg_dq, 3 * hd, i, i + 1)
        elif kind == "nb":
            first_norm_back(int(at))
        elif kind == "if":
            ag_in.forward(int(at))
        elif kind == "fi":
            ag_in.finish(int(at))
        elif token == "sums":
            sums()
        elif token == "sm":
            small_steps.pop(0)()
        elif token == "fo":
            for s in range(parts):
                ag_out.finish(s)

    def run(tokens):
        for token in tokens:
            do(token)

    run(BEFORE_ATTENTION)

    for s in range(parts):
        rows = part_rows(s)

        def back(h, carry, s=s, rows=rows):
            p = probs[h, :, rows]
            low = do_t[h, :, rows]
            wg = mm(rows3[h], low)
            sg = (p.astype(f32) * (wg - delta[h, :, rows])).astype(bf16)
            dv = mm(p, low.astype(f32).T.astype(bf16))
            dk = mm(sg, q_t[h, :, rows].astype(f32).T.astype(bf16))
            do_t[h, :, rows] = (mm(k_t[h], sg) * (1.0 / HEAD_DIM**0.5)).astype(bf16)
            if s == 0:
                acc[h, :, :HEAD_DIM] = dv
                acc[h, :, HEAD_DIM:] = dk
            else:
                acc[h, :, :HEAD_DIM] += dv
                acc[h, :, HEAD_DIM:] += dk
            for k in range(heads - 1):

                @pl.when(h == k)
                def _(k=k):
                    run(IN_ATTENTION[s][k])

            return carry

        lax.fori_loop(0, heads, back, 0)
        run(IN_ATTENTION[s][heads - 1])

    run(AFTER_ATTENTION)
    while small_steps or any(chains.values()):
        for name in ("qa", "qb", "qc", "f2a", "f2b", "f2c", "f1a", "f1b", "f1c", "w"):
            if chains[name]:
                do(name)
        if small_steps:
            do("sm")
    ag_in.finish(parts - 1)


def sincos_rows(feature_count):
    half_width = feature_count // 6
    ladder = np.arange(half_width, dtype=np.float32) / np.float32(half_width)
    frequency = np.power(np.float32(10000.0), -ladder).astype(np.float32)
    angles = (np.arange(COORDS, dtype=np.float32)[:, None] * frequency[None, :]).astype(np.float32)
    wide = angles.astype(np.float64)
    left = np.concatenate([np.sin(wide), np.cos(wide)], axis=1)
    terms = []
    for _ in range(3):
        terms.append(left.astype(np.float32).astype(ml_dtypes.bfloat16))
        left = left - terms[-1].astype(np.float64)
    return jnp.asarray(np.concatenate(terms, axis=0))


def on_device(
    n_dp,
    layer_input,
    patch_coords,
    item_lengths,
    out_grad,
    ln1_gain,
    ln1_shift,
    w_qkv,
    b_qv,
    w_out,
    b_out,
    ln2_gain,
    ln2_shift,
    w_fc1,
    b_fc1,
    w_fc2,
    b_fc2,
):
    tokens, width = layer_input.shape
    hd = w_out.shape[0]
    ff = w_fc1.shape[1]
    heads = hd // HEAD_DIM
    parts = tokens // (4 * BLK)
    log_n = n_dp.bit_length() - 1
    size = 4 * BLK
    got = Reduce.got_rows
    vmem = lambda *s: pltpu.VMEM(s, bf16)
    vmem32 = lambda *s: pltpu.VMEM(s, f32)
    scratch = [
        vmem(tokens, width),
        vmem(tokens, width),
        vmem(tokens, width),
        vmem(heads, HEAD_DIM, tokens),
        vmem(heads, HEAD_DIM, tokens),
        vmem(heads, HEAD_DIM, tokens),
        vmem(heads, tokens, HEAD_DIM),
        vmem(heads, tokens, tokens),
        vmem(parts, 4 * hd, size),
        vmem32(heads, 1, tokens),
        vmem(4 * hd, width),
        vmem(width, ff),
        vmem(ff, width),
        vmem32(parts, BLK, width),
        vmem(tokens, width),
    ]
    for _ in range(2):
        scratch += [
            vmem(parts, 2, 2, BLK, width),
            vmem(parts, 2, BLK, width),
            vmem(parts, BLK, width),
        ]
    scratch += [
        vmem32(parts, BLK, width),
        vmem32(heads, 1, tokens),
        vmem32(heads, tokens, 2 * HEAD_DIM),
        vmem(3 * got(width // 3, 3, log_n), width),
        vmem(3 * got(width // 3, 3, log_n), width),
        vmem(got(hd, 2, log_n), width),
        vmem(3 * got(width // 3, 3, log_n), 3 * hd),
        pltpu.VMEM((tokens, BLK), jnp.int32),
        vmem32(2 + log_n, 16, width),
        vmem32(2 + log_n, 16, width),
        vmem32(8, ff),
    ]
    n_sems = 3 + 4 * 3 * parts + 3 * 2 * parts + 9 * (log_n + 3) + (log_n + 2) + 2 + log_n
    scratch += [
        pltpu.SemaphoreType.DMA((n_sems,)),
        pltpu.SemaphoreType.DMA((n_sems,)),
        pltpu.SemaphoreType.REGULAR((29,)),
        pltpu.SemaphoreType.DMA((4 * parts * 2 + parts + 3 + 10 + 2 + 4 * parts,)),
    ]
    hbm = pl.BlockSpec(memory_space=pl.ANY)
    here = pl.BlockSpec(memory_space=pltpu.VMEM)
    results = pl.pallas_call(
        functools.partial(layer_kernel, (parts, log_n, heads)),
        name="layer",
        out_shape=(
            vmem(tokens, width),
            vmem(tokens, width),
            vmem(ff, width),
            vmem(width, ff),
            vmem(hd, width),
            vmem(width, 3 * hd),
            vmem32(16, width),
        ),
        in_specs=[pl.BlockSpec(memory_space=pltpu.SMEM), hbm, hbm, here, here, hbm, hbm, hbm] + [here] * 9,
        out_specs=(here,) * 7,
        scratch_shapes=scratch,
        compiler_params=pltpu.CompilerParams(
            collective_id=0, has_side_effects=True, vmem_limit_bytes=67043328 - 2 * (2 * tokens * width + 2 * ff * width + 4 * hd * width) - 64 * width - 600000
        ),
    )(
        item_lengths,
        layer_input,
        out_grad,
        patch_coords,
        w_qkv.reshape(width, 3 * hd).T,
        w_out,
        w_fc1,
        w_fc2,
        ln1_gain,
        ln1_shift,
        ln2_gain,
        ln2_shift,
        b_out,
        b_fc2,
        b_fc1,
        b_qv,
        sincos_rows(width),
    )
    layer_output, input_grad, g_fc2, g_fc1, g_wout, g_qkv, small = results
    return (
        layer_output,
        input_grad.astype(f32),
        small[0],
        small[1],
        g_qkv.astype(f32).reshape(width, 3, hd),
        small[9:11, :hd],
        g_wout.astype(f32),
        small[4],
        small[2],
        small[3],
        g_fc1.astype(f32),
        small[8, :ff],
        g_fc2.astype(f32),
        small[5],
    )


def solution(mesh):
    placed = (
        P("dp", None),
        P(None, "dp"),
        P("dp"),
        P("dp", None),
        P(),
        P(),
        P(None, None, "tensor"),
        P(None, "tensor"),
        P("tensor", None),
        P(),
        P(),
        P(),
        P(None, "tensor"),
        P("tensor"),
        P("tensor", None),
        P(),
    )
    return jax.shard_map(
        functools.partial(on_device, mesh.shape["dp"]),
        mesh=mesh,
        in_specs=placed,
        out_specs=(
            P("dp", None),
            P("dp", None),
            P(),
            P(),
            P(None, None, "tensor"),
            P(None, "tensor"),
            P("tensor", None),
            P(),
            P(),
            P(),
            P(None, "tensor"),
            P("tensor"),
            P("tensor", None),
            P(),
        ),
        check_vma=False,
    )
```
